32 devices in a mesh: aux: 16 (over z, y, x), grp: 2 (over core).
Axes of the slice: x: 2, y: 2, z: 4, core: 2. Of those that a mesh axis runs over, the one named last changes fastest.
Arguments:
- integrals: bfloat16 [1024, 16, 4096], P(('aux', 'grp')), may hold values from -6 to 6
- block_pairs: int32 [32, 16, 2], P(('aux', 'grp')), may hold values from 0 to 63
- occupied: bfloat16 [2, 4096], replicated, may hold values from -0.75 to 0.75
- virtual: bfloat16 [4096, 3072], P(None, 'grp'), may hold values from -0.1875 to 0.1875
- stored: bfloat16 [1024, 6144], P('aux'), may hold values from -0.1875 to 0.1875
Outputs:
- exchange_panel: bfloat16 [2, 3072, 2, 3072], P(None, ('grp', 'aux'))
The draws below stay inside these ranges and needn't reach their ends.
Inputs may be any that keep to these rules, and one draw needn't show every extreme that they name: `block_pairs`: block pairs may repeat within a shard; repeated blocks add.
All inputs are finite; a program needn't handle non-finite values.
Results may differ from the reference program's by a relative error of at most 0.0095.
Values may be sent and summed in bfloat16 or wider, within the bound.
A program may use at most 192 MiB of HBM per device.

```python
import jax
import jax.numpy as jnp
from jax import lax

NBAS = 4096
BLK = 64
V = 3072
NOCC = 2
JWIN = 2
AUX_DEV = 32
NB = 16
SHARDS = 32
NAUX = 1024
N_AUX = 16
N_GRP = 2


def place_ends(entries, key, low, largest):
    index_at = [jax.random.randint(jax.random.fold_in(key, axis), (), 0, length) for axis, length in enumerate(entries.shape)]
    widest = entries.shape.index(max(entries.shape))
    neighbour = index_at[:widest] + [(index_at[widest] + 1) % entries.shape[widest]] + index_at[widest + 1:]
    return entries.at[tuple(index_at)].set(low).at[tuple(neighbour)].set(largest)


def block_scale(rng, shape, split, least, high):
    loudness = 1.0
    for dim, blocks in split:
        heights = jax.random.uniform(jax.random.fold_in(jax.random.fold_in(rng, 6), dim), (blocks,), jnp.float32, least / len(split), high / len(split))
        loudness = loudness * jnp.repeat(jnp.exp(heights), shape[dim] // blocks).reshape((-1,) + (1,) * (len(shape) - 1 - dim))
    return loudness


def centred(rng, dims, spread, bound, pieces=(), held_as=jnp.bfloat16):
    values = jax.random.normal(rng, dims, jnp.float32) * spread
    if len(pieces) > 0:
        values = block_scale(rng, dims, pieces, -0.22, 0.18) * values
    return jnp.clip(values, min=-bound, max=bound).astype(held_as)


def setup_inputs(seed: int = 0) -> dict:
    splits = jax.random.split(jax.random.key(seed), 6)
    integrals = centred(splits[0], (NAUX, NB, BLK * BLK), 1.0, 6.0, ((0, 32),))
    block_pairs = place_ends(jax.random.randint(splits[1], (SHARDS, NB, 2), 0, NBAS // BLK), jax.random.fold_in(splits[1], 1), 0, (NBAS // BLK) - 1).astype(jnp.int32)
    occupied = centred(splits[2], (NOCC, NBAS), BLK ** -0.5, 0.75)
    virtual = centred(splits[3], (NBAS, V), (BLK * NB) ** -0.5, 0.1875, ((1, 2),))
    stored = centred(splits[4], (NAUX, JWIN * V), NAUX ** -0.5, 0.1875, ((0, 16),))
    return dict(integrals=integrals, block_pairs=block_pairs, occupied=occupied, virtual=virtual, stored=stored)


def shard_factor(tiles, pairs, occupied, virtual):
    nblocks = NBAS // BLK
    block_iota = jnp.arange(nblocks, dtype=jnp.int32)
    row_pick = (pairs[:, 0:1] == block_iota[None, :]).astype(jnp.float32)
    col_pick = (pairs[:, 1:2] == block_iota[None, :]).astype(jnp.float32)
    occ_blocks = occupied.astype(jnp.float32).reshape(NOCC, nblocks, BLK)
    picked = jnp.einsum('ikm,bk->ibm', occ_blocks, row_pick)
    squares = tiles.astype(jnp.float32).reshape(AUX_DEV, NB, BLK, BLK)
    partial_value = jnp.einsum('ibm,pbmn->pibn', picked, squares)
    half = jnp.einsum('pibn,bk->pikn', partial_value, col_pick).reshape(AUX_DEV * NOCC, NBAS).astype(jnp.bfloat16)
    factor = jnp.dot(half, virtual, preferred_element_type=jnp.float32).astype(jnp.bfloat16)
    return factor.reshape(AUX_DEV, NOCC, V).transpose(0, 2, 1).reshape(AUX_DEV, V * NOCC)


def reference(integrals, block_pairs, occupied, virtual, stored):
    shard_count = N_AUX * N_GRP
    tiles_all = integrals.reshape(shard_count, AUX_DEV, NB, BLK * BLK)
    stored_all = stored.reshape(shard_count, AUX_DEV, JWIN * V)

    def step(carry, inputs):
        tiles, pairs, rows = inputs
        factor = shard_factor(tiles, pairs, occupied, virtual)
        term = lax.dot_general(factor, rows, (((0,), (0,)), ((), ())), preferred_element_type=jnp.float32)
        return carry + term, None

    start = jnp.zeros((V * NOCC, JWIN * V), jnp.float32)
    total, unused = lax.scan(step, start, (tiles_all, block_pairs, stored_all))
    result = total.astype(jnp.bfloat16).reshape(V, NOCC, JWIN, V)
    return result.transpose(1, 0, 2, 3)
```

```python
import functools
import math

import jax
import jax.numpy as jnp
from jax import lax
from jax.experimental import pallas as pl
from jax.experimental.pallas import tpu as pltpu
from jax.sharding import PartitionSpec as P

MESH = pl.DeviceIdType.MESH
LANES = 128
PLANE = 4
PIECES = 3
FIRST = 1


def spans_of(width):
    piece = width // PIECES // LANES * LANES
    starts = [n * piece for n in range(PIECES)] + [width]
    return [(a, b - a, 0 if n < FIRST else 1) for n, (a, b) in enumerate(zip(starts, starts[1:]))]


def weigh(pairs, occ, weights):
    nb = pairs.shape[0]
    nocc, nblocks, blk = occ.shape
    lanes = lax.broadcasted_iota(jnp.int32, (nb, nblocks), 1)
    pick = (pairs[:, 0:1] == lanes).astype(jnp.bfloat16)
    step = 8 * LANES
    row = lax.broadcasted_iota(jnp.int32, (blk, step), 0) * blk
    col = lax.broadcasted_iota(jnp.int32, (blk, step), 1)
    for i in range(nocc):
        picked = jnp.dot(pick, occ[i], preferred_element_type=jnp.float32).astype(jnp.bfloat16)
        for t in range(weights.shape[2] // step):
            offset = col + t * step - row
            spread = ((offset >= 0) & (offset < blk)).astype(jnp.bfloat16)
            weights[i, :, t * step:(t + 1) * step] = jnp.dot(
                picked, spread, preferred_element_type=jnp.float32)


def contract(blk, integrals, weights, part):
    aux_rows = integrals.shape[0]
    nocc = weights.shape[0]

    @pl.loop(0, aux_rows)
    def _(p):
        for i in range(nocc):
            sums = [None, None]
            for t in range(integrals.shape[2] // LANES):
                cols = slice(t * LANES, (t + 1) * LANES)
                term = integrals[p, :, cols].astype(jnp.float32) * weights[i, :, cols]
                sums[t % 2] = term if sums[t % 2] is None else sums[t % 2] + term
            total = sums[0] + sums[1]
            whole = total
            for f in range(1, LANES // blk):
                whole = whole + pltpu.roll(total, f * blk, 1)
            part[i * aux_rows + p] = whole


def place(blk, pairs, part, turned, half, grp):
    nb = pairs.shape[0]
    per = LANES // blk
    for k in range(nb):
        turned[k] = part[:, k, :]
    lane = lax.broadcasted_iota(jnp.int32, (1, LANES), 1) // blk

    @pl.loop(0, half.shape[2] // LANES)
    def _(b):
        here = lane + b * per
        total = None
        for k in range(nb):
            term = jnp.where(here == pairs[k:k + 1, 1:2], turned[k], 0.0)
            total = term if total is None else total + term
        half[grp, :, pl.ds(pl.multiple_of(b * LANES, LANES), LANES)] = total.astype(half.dtype)


def multiply(nocc, local, half, virt, chunk):
    n_grp, both, nbas = half.shape
    aux_rows = both // nocc
    step = math.lcm(local, LANES)
    for t in range(virt.shape[1] // step):
        product = jnp.dot(
            half[...].reshape(n_grp * both, nbas), virt[:, t * step:(t + 1) * step],
            preferred_element_type=jnp.float32)
        for c in range(step // local):
            d = t * (step // local) + c
            for q in range(n_grp):
                for i in range(nocc):
                    top = q * both + i * aux_rows
                    chunk[d, q * aux_rows:(q + 1) * aux_rows, i * local:(i + 1) * local] = product[
                        top:top + aux_rows, c * local:(c + 1) * local].astype(chunk.dtype)


def panel_any_kernel(n_aux, n_grp, integrals, pairs_in, occ, virtual, stored, out, rows, fac, total, block,
                 ints, virt, weights, part, turned, half, chunk,
                 own_sem, recv, send, frecv, fsend, precv, psend, orecv, osend, hrecv, hsend):
    me = lax.axis_index("aux")
    grp = lax.axis_index("grp")
    line = n_aux // PLANE
    width = rows.shape[2]
    spans = spans_of(width)
    z = me // PLANE
    su = 1 + grp % 2
    sv = 3 - su
    u = (me // su) % 2
    v = (me // sv) % 2
    next_u = me + su * (1 - 2 * u)
    next_v = me + sv * (1 - 2 * v)
    up, down = z + 1 < line, z >= 1
    targets = {"up": me + PLANE, "down": me - PLANE, "u": next_u, "v": next_v}
    slots = {"up": 0, "down": 1, "u": 2, "v": 3}

    load = pltpu.make_async_copy(
        stored.at[:, pl.ds(pl.multiple_of(grp * width, LANES), width)], rows.at[me], own_sem.at[0])
    load.start()
    mine = pltpu.make_async_copy(chunk.at[me], fac.at[grp, me], own_sem.at[1])
    load_ints = pltpu.make_async_copy(integrals, ints, own_sem.at[3])
    load_ints.start()
    load_virt = pltpu.make_async_copy(virtual, virt, own_sem.at[4])
    load_virt.start()
    pairs = pairs_in.at[0]
    nocc, nblocks, blk = occ.shape
    local = virtual.shape[1] // n_aux

    barrier = pltpu.get_barrier_semaphore()
    for o in range(1, n_aux):
        pl.semaphore_signal(barrier, inc=1, device_id=(lax.rem(me + o, n_aux), grp), device_id_type=MESH)
    for o in range(1, n_grp):
        pl.semaphore_signal(barrier, inc=1, device_id=(me, lax.rem(grp + o, n_grp)), device_id_type=MESH)
    pl.semaphore_wait(barrier, n_aux - 1 + n_grp - 1)

    def copy(source, colour, way):
        at = rows.at[source, :, pl.ds(*spans[colour][:2])]
        return pltpu.make_async_remote_copy(
            src_ref=at, dst_ref=at,
            send_sem=send.at[colour, slots[way], source], recv_sem=recv.at[colour, source],
            device_id=(targets[way], grp), device_id_type=MESH)

    def when(condition, action):
        if condition is None:
            action()
        else:
            pl.when(condition)(action)

    edges = {"up": up, "down": down, "u": None, "v": None}

    def ways_of(dz, du, dv, colour):
        if dv:
            return ()
        along = ("up", "down") if dz == 0 else (("up",) if dz > 0 else ("down",))
        if colour == 0:
            return ("v",) if du else along + ("u", "v")
        if dz == 0 and du == 0:
            return ("u",) + along + ("v",)
        return along + ("v",)

    def source_of(dz, du, dv):
        return (z - dz) * PLANE + su * (u + du * (1 - 2 * u)) + sv * (v + dv * (1 - 2 * v))

    def valid(dz):
        if dz == 0:
            return None
        return z - dz >= 0 if dz > 0 else z - dz < line

    sent = []

    def forward(dz, du, dv):
        source = source_of(dz, du, dv)
        for colour in range(len(spans)):
            ways = ways_of(dz, du, dv, spans[colour][2])
            sent.append((dz, source, colour, ways))

            def act(colour=colour, ways=ways):
                if (dz, du, dv) != (0, 0, 0):
                    copy(source, colour, "v").wait_recv()
                for way in ways:
                    when(edges[way], copy(source, colour, way).start)

            when(valid(dz), act)

    def plane_dot(dz, first):
        def act():
            base = (z - dz) * PLANE
            tile = 512 if width % 512 == 0 else LANES

            @pl.loop(0, width // tile)
            def _(t):
                cols = pl.ds(pl.multiple_of(t * tile, tile), tile)
                right = rows[pl.ds(base, PLANE), :, cols].reshape(-1, tile)
                for q in range(n_grp):
                    left = fac[q, pl.ds(base, PLANE)].reshape(-1, fac.shape[3])
                    term = lax.dot_general(
                        left, right, (((0,), (0,)), ((), ())), preferred_element_type=jnp.float32)
                    if first:
                        total[q, :, cols] = term
                    else:
                        total[q, :, cols] += term

        when(valid(dz), act)

    offsets = [(dz, du, dv) for dz in range(1 - line, line) for du in (0, 1) for dv in (0, 1)]
    hops = lambda o: abs(o[0]) + o[1] + o[2]
    last_hop = line + 1

    def fac_copy(o):
        to = lax.rem(me + o, n_aux)
        return pltpu.make_async_remote_copy(
            src_ref=chunk.at[to], dst_ref=fac.at[grp, me], send_sem=fsend.at[o], recv_sem=frecv.at[o],
            device_id=(to, grp), device_id_type=MESH)

    def fac_wait(o):
        source = lax.rem(me + n_aux - o, n_aux)
        pltpu.make_async_remote_copy(
            src_ref=chunk.at[0], dst_ref=fac.at[grp, source], send_sem=fsend.at[o], recv_sem=frecv.at[o],
            device_id=(source, grp), device_id_type=MESH).wait_recv()
        return source

    def share(o, source, p):
        return pltpu.make_async_remote_copy(
            src_ref=fac.at[grp, source], dst_ref=fac.at[grp, source],
            send_sem=psend.at[p, o], recv_sem=precv.at[p, o],
            device_id=(me, lax.rem(grp + p, n_grp)), device_id_type=MESH)

    def half_copy(p):
        return pltpu.make_async_remote_copy(
            src_ref=half.at[grp], dst_ref=half.at[grp], send_sem=hsend.at[p], recv_sem=hrecv.at[p],
            device_id=(me, lax.rem(grp + p, n_grp)), device_id_type=MESH)

    for hop in range(last_hop + 1):
        if hop == 0:
            load.wait()
        for offset in offsets:
            if hops(offset) == hop:
                forward(*offset)
        if hop == 0:
            weigh(pairs, occ, weights)
            load_ints.wait()
            contract(blk, ints, weights, part)
            place(blk, pairs, part, turned, half, grp)
            for p in range(1, n_grp):
                half_copy(p).start()
        if hop == 1:
            for p in range(1, n_grp):
                giver = lax.rem(grp + n_grp - p, n_grp)
                pltpu.make_async_remote_copy(
                    src_ref=half.at[giver], dst_ref=half.at[giver], send_sem=hsend.at[p],
                    recv_sem=hrecv.at[p], device_id=(me, giver), device_id_type=MESH).wait_recv()
            load_virt.wait()
            multiply(nocc, local, half, virt, chunk)
            mine.start()
            for o in range(1, n_aux):
                fac_copy(o).start()
            mine.wait()
        if hop == 2:
            for o in range(n_aux):
                source = me if o == 0 else fac_wait(o)
                for p in range(1, n_grp):
                    share(o, source, p).start()
            for o in range(n_aux):
                source = lax.rem(me + n_aux - o, n_aux)
                for p in range(1, n_grp):
                    giver = lax.rem(grp + n_grp - p, n_grp)
                    pltpu.make_async_remote_copy(
                        src_ref=fac.at[grp, source], dst_ref=fac.at[giver, source],
                        send_sem=psend.at[p, o], recv_sem=precv.at[p, o],
                        device_id=(me, giver), device_id_type=MESH).wait_recv()
        if hop >= 2:
            for dz in sorted({hop - 2, 2 - hop}):
                plane_dot(dz, hop == 2)

    def give(p, n):
        to = lax.rem(grp + p, n_grp)
        cols = pl.ds(*spans[n][:2])
        return pltpu.make_async_remote_copy(
            src_ref=block.at[to, :, cols], dst_ref=out.at[grp, :, cols],
            send_sem=osend.at[p, n], recv_sem=orecv.at[p, n],
            device_id=(me, to), device_id_type=MESH)

    for p in range(1, n_grp):
        to = lax.rem(grp + p, n_grp)
        for n in range(len(spans)):
            cols = pl.ds(*spans[n][:2])
            block[to, :, cols] = total[to, :, cols].astype(block.dtype)
            give(p, n).start()
    block[grp] = total[grp].astype(block.dtype)
    keep = pltpu.make_async_copy(block.at[grp], out.at[grp], own_sem.at[2])
    keep.start()

    for dz, source, colour, ways in sent:
        def drain(source=source, colour=colour, ways=ways):
            for way in ways:
                when(edges[way], copy(source, colour, way).wait_send)
        if ways:
            when(valid(dz), drain)
    for p in range(1, n_grp):
        half_copy(p).wait_send()
    for o in range(1, n_aux):
        fac_copy(o).wait_send()
    for o in range(n_aux):
        source = lax.rem(me + n_aux - o, n_aux)
        for p in range(1, n_grp):
            share(o, source, p).wait_send()
    for p in range(1, n_grp):
        giver = lax.rem(grp + n_grp - p, n_grp)
        for n in range(len(spans)):
            cols = pl.ds(*spans[n][:2])
            give(p, n).wait_send()
            pltpu.make_async_remote_copy(
                src_ref=block.at[giver, :, cols], dst_ref=out.at[giver, :, cols],
                send_sem=osend.at[p, n], recv_sem=orecv.at[p, n],
                device_id=(me, giver), device_id_type=MESH).wait_recv()
    keep.wait()


def panels_any(integrals, pairs, occ, virtual, stored, n_aux, n_grp):
    depth = stored.shape[0]
    width = stored.shape[1] // n_grp
    aux_rows, nb, flat = integrals.shape
    nocc, nblocks, blk = occ.shape
    nbas, slab = virtual.shape
    pieces = len(spans_of(width))
    cols = nocc * (slab // n_aux)
    dma = pltpu.SemaphoreType.DMA
    hbm = pl.BlockSpec(memory_space=pltpu.HBM)
    vmem = pl.BlockSpec(memory_space=pltpu.VMEM)
    return pl.pallas_call(
        functools.partial(panel_any_kernel, n_aux, n_grp),
        out_shape=jax.ShapeDtypeStruct((n_grp, cols, width), jnp.bfloat16),
        in_specs=[hbm, vmem, vmem, hbm, hbm],
        out_specs=hbm,
        scratch_shapes=[
            pltpu.VMEM((n_aux, depth, width), jnp.bfloat16),
            pltpu.VMEM((n_grp, n_aux, depth, cols), jnp.bfloat16),
            pltpu.VMEM((n_grp, cols, width), jnp.float32),
            pltpu.VMEM((n_grp, cols, width), jnp.bfloat16),
            pltpu.VMEM(integrals.shape, jnp.bfloat16),
            pltpu.VMEM(virtual.shape, jnp.bfloat16),
            pltpu.VMEM((nocc, nb, flat), jnp.float32),
            pltpu.VMEM((nocc * aux_rows, nb, LANES), jnp.float32),
            pltpu.VMEM((nb, nocc * aux_rows, LANES), jnp.float32),
            pltpu.VMEM((n_grp, nocc * aux_rows, nbas), jnp.bfloat16),
            pltpu.VMEM((n_aux, depth, cols), jnp.bfloat16),
            dma((5,)),
            dma((pieces, n_aux)),
            dma((pieces, 4, n_aux)),
            dma((n_aux,)),
            dma((n_aux,)),
            dma((n_grp, n_aux)),
            dma((n_grp, n_aux)),
            dma((n_grp, pieces)),
            dma((n_grp, pieces)),
            dma((n_grp,)),
            dma((n_grp,)),
        ],
        compiler_params=pltpu.CompilerParams(
            collective_id=0, has_side_effects=True, vmem_limit_bytes=63 * 1024 * 1024),
    )(integrals, pairs, occ, virtual, stored)


def weigh_blocks(pairs, occ, weights):
    nocc, nbas = occ.shape
    nb = pairs.shape[1]
    blk = math.isqrt(weights.shape[2])
    per = LANES // blk
    tiles = nbas // LANES
    line = lax.broadcasted_iota(jnp.int32, (tiles, nb), 0) * per
    step = 8 * LANES
    row = lax.broadcasted_iota(jnp.int32, (blk, step), 0) * blk
    col = lax.broadcasted_iota(jnp.int32, (blk, step), 1)
    orbital = occ[...].astype(jnp.float32)
    for i in range(nocc):
        table = jnp.concatenate(
            [orbital[i:i + 1, t * LANES:(t + 1) * LANES] for t in range(tiles)], axis=0).astype(jnp.bfloat16)
        picked = None
        for f in range(per):
            pick = (pairs[0:1, :] == line + f).astype(jnp.bfloat16)
            term = lax.dot_general(
                pick, table[:, f * blk:(f + 1) * blk], (((0,), (0,)), ((), ())), preferred_element_type=jnp.float32)
            picked = term if picked is None else picked + term
        picked = picked.astype(jnp.bfloat16)
        for t in range(weights.shape[2] // step):
            offset = col + t * step - row
            spread = ((offset >= 0) & (offset < blk)).astype(jnp.bfloat16)
            weights[i, :, t * step:(t + 1) * step] = jnp.dot(
                picked, spread, preferred_element_type=jnp.float32)


def compact(blk, part, half, grp):
    nb = part.shape[1]
    per = LANES // blk
    lane = lax.broadcasted_iota(jnp.int32, (part.shape[0], LANES), 1) // blk
    for t in range(nb // per):
        tile = part[:, t * per, :]
        for f in range(1, per):
            tile = jnp.where(lane == f, part[:, t * per + f, :], tile)
        half[grp, :, t * LANES:(t + 1) * LANES] = tile.astype(half.dtype)


def expand(nocc, local, blk, index, half, virt, chunk):
    n_grp, both, depth = half.shape
    aux_rows = both // nocc
    wide = 2 * local
    step = math.lcm(wide, 2 * LANES)
    for q in range(n_grp):
        for t in range(virt.shape[2] // step):
            cols = slice(t * step, (t + 1) * step)
            right = jnp.concatenate([virt[index[q, 1, k], :, cols] for k in range(depth // blk)], axis=0)
            product = jnp.dot(half[q], right, preferred_element_type=jnp.float32).astype(chunk.dtype)
            for c in range(step // wide):
                for i in range(nocc):
                    chunk[t * (step // wide) + c, q * aux_rows:(q + 1) * aux_rows, i * wide:(i + 1) * wide] = product[
                        i * aux_rows:(i + 1) * aux_rows, c * wide:(c + 1) * wide]


def panel_kernel(n_aux, v, piece, integrals, pairs_in, occ_in, virtual, stored, out, rows, fac, turned, block,
                 ints, virt, weights, part, half, chunk, pairs, index, occ,
                 load_sem, own_sem, xsend, xrecv, send, recv, hsend, hrecv, fsend, frecv, gsend, grecv, psend, precv,
                 osend, orecv):
    me = lax.axis_index("aux")
    grp = lax.axis_index("grp")
    other = 1 - grp
    line = n_aux // PLANE
    nj = stored.shape[1] // v
    quarter = v // 4
    pieces = quarter // piece
    nocc = occ.shape[0]
    blk = math.isqrt(integrals.shape[2])
    local = virtual.shape[2] // n_aux
    z = me // PLANE
    x = me % 2
    y = (me // 2) % 2
    pair = me // 2
    n_pairs = n_aux // 2
    xmate = me + 1 - 2 * x
    ymate = me + 2 * (1 - 2 * y)
    targets = {"up": me + PLANE, "down": me - PLANE, "y": ymate}
    slots = {"up": 0, "down": 1, "y": 2}
    edges = {"up": z + 1 < line, "down": z >= 1, "y": None}
    mine = 2 * x + grp
    theirs = 2 * (1 - x) + grp

    def column(j, q, n):
        return pl.ds(pl.multiple_of(j * v + q * quarter + n * piece, LANES), piece)

    load_pairs = pltpu.make_async_copy(pairs_in.at[0], pairs.at[grp], load_sem.at[0])
    load_pairs.start()
    load_occ = pltpu.make_async_copy(occ_in, occ, load_sem.at[1])
    load_occ.start()
    load_ints = pltpu.make_async_copy(integrals, ints, load_sem.at[2])
    load_ints.start()
    for n in range(pieces):
        for j in range(nj):
            pltpu.make_async_copy(
                stored.at[:, column(j, mine, n)], rows.at[n, me, :, pl.ds(j * piece, piece)], own_sem.at[n, j]).start()
    load_virt = pltpu.make_async_copy(virtual, virt, load_sem.at[3])
    load_virt.start()

    barrier = pltpu.get_barrier_semaphore()
    peers = [((pair + o) % n_pairs * 2 + x, grp) for o in range(1, n_pairs)]
    peers += [(xmate, grp), (xmate, other), (me, other)]
    for peer in peers:
        pl.semaphore_signal(barrier, inc=1, device_id=peer, device_id_type=MESH)

    def when(condition, action):
        if condition is None:
            action()
        else:
            pl.when(condition)(action)

    def remote(src, dst, send_sem, recv_sem, device):
        return pltpu.make_async_remote_copy(
            src_ref=src, dst_ref=dst, send_sem=send_sem, recv_sem=recv_sem, device_id=device, device_id_type=MESH)

    def copy(n, source, way):
        at = rows.at[n, source]
        return remote(at, at, send.at[n, slots[way], source], recv.at[n, source], (targets[way], grp))

    def cross(n, j):
        return remote(
            stored.at[:, column(j, theirs, n)], rows.at[n, me, :, pl.ds(j * piece, piece)],
            xsend.at[n, j], xrecv.at[n, j], (xmate, grp))

    def cross_wait(n, j):
        at = rows.at[n, xmate, :, pl.ds(j * piece, piece)]
        remote(at, at, xsend.at[n, j], xrecv.at[n, j], (xmate, grp)).wait_recv()

    def valid(dz):
        if dz == 0:
            return None
        return z - dz >= 0 if dz > 0 else z - dz < line

    sent = []

    def forward(n, dz, far):
        source = (z - dz) * PLANE + y * 2 + (1 - x if far else x)
        ways = ("up", "down", "y") if dz == 0 else (("up", "y") if dz > 0 else ("down", "y"))
        sent.append((n, dz, source, ways))

        def act():
            if dz == 0:
                for j in range(nj):
                    if far:
                        cross_wait(n, j)
                    else:
                        at = rows.at[n, me, :, pl.ds(j * piece, piece)]
                        pltpu.make_async_copy(stored.at[:, column(j, mine, n)], at, own_sem.at[n, j]).wait()
            else:
                copy(n, source, "y").wait_recv()
            for way in ways:
                when(edges[way], copy(n, source, way).start)

        when(valid(dz), act)

    def stage(group, distance, far):
        for n in group:
            for dz in sorted({distance, -distance}):
                forward(n, dz, far)

    def half_copy():
        return remote(half.at[grp], half.at[grp], hsend.at[0], hrecv.at[0], (me, other))

    def pairs_copy():
        return remote(pairs.at[grp], pairs.at[grp], hsend.at[1], hrecv.at[1], (me, other))

    def fac_copy(o):
        to = (pair + o) % n_pairs
        return remote(chunk.at[to], fac.at[grp, me], fsend.at[o], frecv.at[o], (to * 2 + x, grp))

    def fac_source(o):
        return (pair + n_pairs - o) % n_pairs * 2

    def fac_cross(o):
        source = fac_source(o) + x
        return remote(fac.at[grp, source], fac.at[grp, source], gsend.at[o], grecv.at[o], (xmate, grp))

    def share(o, far):
        source = fac_source(o) + (1 - x if far else x)
        return remote(
            fac.at[grp, source], fac.at[grp, source], psend.at[int(far), o], precv.at[int(far), o], (me, other))

    def give(n, rel, q, j):
        to = (grp + q) % 2
        chip = 1 - x if rel else x
        at = xmate if rel else me
        src = block.at[n, to, chip, :, pl.ds(j * piece, piece)]
        dst = out.at[j, :, column(0, mine, n)]
        if not rel and not q:
            return pltpu.make_async_copy(src, dst, osend.at[n, 0, j])
        return remote(src, dst, osend.at[n, 2 * rel + q, j], orecv.at[n, 2 * rel + q, j], (at, to))

    def taken(n, rel, q, j):
        source = 2 * (1 - x if rel else x) + (grp + q) % 2
        dst = out.at[j, :, column(0, source, n)]
        src = block.at[n, 0, 0, :, pl.ds(j * piece, piece)]
        return remote(src, dst, osend.at[n, 2 * rel + q, j], orecv.at[n, 2 * rel + q, j], (xmate, grp))

    def finish(n):
        for dz in range(1 - line, line):
            for far in (0, 1):
                source = (z - dz) * PLANE + (1 - y) * 2 + far

                def arrive(source=source):
                    copy(n, source, "y").wait_recv()

                when(valid(dz), arrive)
        right = rows[n].reshape(-1, nj * piece)
        for q in range(2):
            term = jnp.dot(turned[q], right, preferred_element_type=jnp.float32).astype(block.dtype)
            for i in range(nocc):
                for chip in range(2):
                    top = (i * 2 + chip) * local
                    block[n, q, chip, i * local:(i + 1) * local] = term[top:top + local]
        for rel, q in ((1, 0), (1, 1), (0, 1), (0, 0)):
            for j in range(nj):
                give(n, rel, q, j).start()

    first = list(range((pieces + 1) // 2))
    last = list(range((pieces + 1) // 2, pieces))
    far_hops = range(2, line)

    load_pairs.wait()
    load_occ.wait()
    weigh_blocks(pairs[grp], occ, weights)
    load_ints.wait()
    contract(blk, ints, weights, part)
    pl.semaphore_wait(barrier, len(peers))
    pairs_copy().start()
    for n in range(pieces):
        for j in range(nj):
            cross(n, j).start()
    stage(first, 0, False)
    compact(blk, part, half, grp)
    half_copy().start()
    remote(pairs.at[other], pairs.at[other], hsend.at[1], hrecv.at[1], (me, other)).wait_recv()
    load_index = pltpu.make_async_copy(pairs, index, load_sem.at[0])
    load_index.start()
    stage(first, 0, True)
    load_index.wait()
    load_virt.wait()
    remote(half.at[other], half.at[other], hsend.at[0], hrecv.at[0], (me, other)).wait_recv()
    expand(nocc, local, blk, index, half, virt, chunk)
    for o in range(1, n_pairs):
        fac_copy(o).start()
    keep = pltpu.make_async_copy(chunk.at[pair], fac.at[grp, me], load_sem.at[1])
    keep.start()
    stage(first, 1, False)
    stage(first, 1, True)
    stage(last, 0, False)
    keep.wait()
    for o in range(n_pairs):
        if o:
            source = fac_source(o) + x
            remote(fac.at[grp, source], fac.at[grp, source], fsend.at[o], frecv.at[o], (source, grp)).wait_recv()
        fac_cross(o).start()
        share(o, False).start()
    for hop in far_hops:
        stage(first, hop, False)
        stage(first, hop, True)
    stage(last, 0, True)
    for o in range(n_pairs):
        source = fac_source(o) + 1 - x
        remote(fac.at[grp, source], fac.at[grp, source], gsend.at[o], grecv.at[o], (xmate, grp)).wait_recv()
        share(o, True).start()
    stage(last, 1, False)
    stage(last, 1, True)
    for far in (False, True):
        for o in range(n_pairs):
            source = fac_source(o) + (1 - x if far else x)
            at = fac.at[other, source]
            remote(at, at, psend.at[int(far), o], precv.at[int(far), o], (me, other)).wait_recv()
    group = LANES // fac.shape[2]
    for q in range(2):
        for t in range(n_aux // group):
            turned[q, :, t * LANES:(t + 1) * LANES] = fac[q, t * group:(t + 1) * group].reshape(LANES, -1).T
    for n in first:
        finish(n)
    for hop in far_hops:
        stage(last, hop, False)
        stage(last, hop, True)
    for n in last:
        finish(n)

    for n, dz, source, ways in sent:
        def drain(n=n, source=source, ways=ways):
            for way in ways:
                when(edges[way], copy(n, source, way).wait_send)
        when(valid(dz), drain)
    for n in range(pieces):
        for j in range(nj):
            cross(n, j).wait_send()
    half_copy().wait_send()
    pairs_copy().wait_send()
    for o in range(n_pairs):
        if o:
            fac_copy(o).wait_send()
        fac_cross(o).wait_send()
        share(o, False).wait_send()
        share(o, True).wait_send()
    for n in range(pieces):
        for j in range(nj):
            for rel, q in ((1, 0), (1, 1), (0, 1)):
                give(n, rel, q, j).wait_send()
                taken(n, rel, q, j).wait_recv()
            give(n, 0, 0, j).wait()


def panels(integrals, pairs, occupied, virtual, stored, n_aux, v):
    depth = stored.shape[0]
    aux_rows, nb, flat = integrals.shape
    nocc = occupied.shape[0]
    blk = math.isqrt(flat)
    slab = virtual.shape[2]
    nj = stored.shape[1] // v
    piece = LANES
    pieces = v // 4 // piece
    cols = nocc * (slab // n_aux)
    line = n_aux // PLANE
    n_pairs = n_aux // 2
    dma = pltpu.SemaphoreType.DMA
    hbm = pl.BlockSpec(memory_space=pltpu.HBM)
    return pl.pallas_call(
        functools.partial(panel_kernel, n_aux, v, piece),
        out_shape=jax.ShapeDtypeStruct((nj, cols, v), jnp.bfloat16),
        in_specs=[hbm] * 5,
        out_specs=hbm,
        scratch_shapes=[
            pltpu.VMEM((pieces, n_aux, depth, nj * piece), jnp.bfloat16),
            pltpu.VMEM((2, n_aux, depth, 2 * cols), jnp.bfloat16),
            pltpu.VMEM((2, 2 * cols, n_aux * depth), jnp.bfloat16),
            pltpu.VMEM((pieces, 2, 2, cols, nj * piece), jnp.bfloat16),
            pltpu.VMEM(integrals.shape, jnp.bfloat16),
            pltpu.VMEM(virtual.shape, jnp.bfloat16),
            pltpu.VMEM((nocc, nb, flat), jnp.float32),
            pltpu.VMEM((nocc * aux_rows, nb, LANES), jnp.float32),
            pltpu.VMEM((2, nocc * aux_rows, nb * blk), jnp.bfloat16),
            pltpu.VMEM((n_pairs, depth, 2 * cols), jnp.bfloat16),
            pltpu.VMEM((2, 2, nb), jnp.int32),
            pltpu.SMEM((2, 2, nb), jnp.int32),
            pltpu.VMEM(occupied.shape, jnp.bfloat16),
            dma((4,)),
            dma((pieces, nj)),
            dma((pieces, nj)),
            dma((pieces, nj)),
            dma((pieces, 3, n_aux)),
            dma((pieces, n_aux)),
            dma((2,)),
            dma((2,)),
            dma((n_pairs,)),
            dma((n_pairs,)),
            dma((n_pairs,)),
            dma((n_pairs,)),
            dma((2, n_pairs)),
            dma((2, n_pairs)),
            dma((pieces, 4, nj)),
            dma((pieces, 4, nj)),
        ],
        compiler_params=pltpu.CompilerParams(
            collective_id=0, has_side_effects=True, vmem_limit_bytes=63 * 1024 * 1024),
    )(integrals, pairs, occupied, virtual, stored)


def make_per_device(n_aux, n_grp, v):
    def per_device(integrals, block_pairs, occupied, virtual, stored):
        nocc, nbas = occupied.shape
        local = virtual.shape[1] // n_aux
        blk = math.isqrt(integrals.shape[2])
        if n_grp == 2 and n_aux % PLANE == 0 and v % (4 * LANES) == 0 and LANES % stored.shape[0] == 0:
            panel = panels(integrals, block_pairs.transpose(0, 2, 1), occupied,
                           virtual.reshape(nbas // blk, blk, -1), stored, n_aux, v)
            return panel.transpose(1, 0, 2).reshape(nocc, local, panel.shape[0], v)
        occ = occupied.reshape(nocc, nbas // blk, blk)
        panel = panels_any(integrals, block_pairs, occ, virtual, stored, n_aux, n_grp)
        return panel.transpose(1, 0, 2).reshape(nocc, local, n_grp * panel.shape[2] // v, v)

    return per_device


def solution(mesh):
    n_aux, n_grp = mesh.shape["aux"], mesh.shape["grp"]

    def whole(integrals, block_pairs, occupied, virtual, stored):
        return jax.shard_map(
            make_per_device(n_aux, n_grp, virtual.shape[1]),
            mesh=mesh,
            in_specs=(
                P(("aux", "grp"), None, None),
                P(("aux", "grp"), None, None),
                P(),
                P(None, "grp"),
                P("aux", None),
            ),
            out_specs=P(None, ("grp", "aux"), None, None),
            check_vma=False,
        )(integrals, block_pairs, occupied, virtual, stored)

    return whole
```

```python
import functools
import math

import jax
import jax.numpy as jnp
from jax import lax
from jax.experimental import pallas as pl
from jax.experimental.pallas import tpu as pltpu
from jax.sharding import PartitionSpec as P

MESH = pl.DeviceIdType.MESH
LANES = 128
PLANE = 4
PIECES = 3
FIRST = 1


def spans_of(width):
    piece = width // PIECES // LANES * LANES
    starts = [n * piece for n in range(PIECES)] + [width]
    return [(a, b - a, 0 if n < FIRST else 1) for n, (a, b) in enumerate(zip(starts, starts[1:]))]


def weigh(pairs, occ, weights):
    nb = pairs.shape[0]
    nocc, nblocks, blk = occ.shape
    lanes = lax.broadcasted_iota(jnp.int32, (nb, nblocks), 1)
    pick = (pairs[:, 0:1] == lanes).astype(jnp.bfloat16)
    step = 8 * LANES
    row = lax.broadcasted_iota(jnp.int32, (blk, step), 0) * blk
    col = lax.broadcasted_iota(jnp.int32, (blk, step), 1)
    for i in range(nocc):
        picked = jnp.dot(pick, occ[i], preferred_element_type=jnp.float32).astype(jnp.bfloat16)
        for t in range(weights.shape[2] // step):
            offset = col + t * step - row
            spread = ((offset >= 0) & (offset < blk)).astype(jnp.bfloat16)
            weights[i, :, t * step:(t + 1) * step] = jnp.dot(
                picked, spread, preferred_element_type=jnp.float32)


def contract(blk, integrals, weights, part):
    aux_rows = integrals.shape[0]
    nocc = weights.shape[0]

    @pl.loop(0, aux_rows)
    def _(p):
        for i in range(nocc):
            sums = [None, None]
            for t in range(integrals.shape[2] // LANES):
                cols = slice(t * LANES, (t + 1) * LANES)
                term = integrals[p, :, cols].astype(jnp.float32) * weights[i, :, cols]
                sums[t % 2] = term if sums[t % 2] is None else sums[t % 2] + term
            total = sums[0] + sums[1]
            whole = total
            for f in range(1, LANES // blk):
                whole = whole + pltpu.roll(total, f * blk, 1)
            part[i * aux_rows + p] = whole


def place(blk, pairs, part, turned, half, grp):
    nb = pairs.shape[0]
    per = LANES // blk
    for k in range(nb):
        turned[k] = part[:, k, :]
    lane = lax.broadcasted_iota(jnp.int32, (1, LANES), 1) // blk

    @pl.loop(0, half.shape[2] // LANES)
    def _(b):
        here = lane + b * per
        total = None
        for k in range(nb):
            term = jnp.where(here == pairs[k:k + 1, 1:2], turned[k], 0.0)
            total = term if total is None else total + term
        half[grp, :, pl.ds(pl.multiple_of(b * LANES, LANES), LANES)] = total.astype(half.dtype)


def multiply(nocc, local, half, virt, chunk):
    n_grp, both, nbas = half.shape
    aux_rows = both // nocc
    step = math.lcm(local, LANES)
    for t in range(virt.shape[1] // step):
        product = jnp.dot(
            half[...].reshape(n_grp * both, nbas), virt[:, t * step:(t + 1) * step],
            preferred_element_type=jnp.float32)
        for c in range(step // local):
            d = t * (step // local) + c
            for q in range(n_grp):
                for i in range(nocc):
                    top = q * both + i * aux_rows
                    chunk[d, q * aux_rows:(q + 1) * aux_rows, i * local:(i + 1) * local] = product[
                        top:top + aux_rows, c * local:(c + 1) * local].astype(chunk.dtype)


def panel_any_kernel(n_aux, n_grp, integrals, pairs_in, occ, virtual, stored, out, rows, fac, total, block,
                 ints, virt, weights, part, turned, half, chunk,
                 own_sem, recv, send, frecv, fsend, precv, psend, orecv, osend, hrecv, hsend):
    me = lax.axis_index("aux")
    grp = lax.axis_index("grp")
    line = n_aux // PLANE
    width = rows.shape[2]
    spans = spans_of(width)
    z = me // PLANE
    su = 1 + grp % 2
    sv = 3 - su
    u = (me // su) % 2
    v = (me // sv) % 2
    next_u = me + su * (1 - 2 * u)
    next_v = me + sv * (1 - 2 * v)
    up, down = z + 1 < line, z >= 1
    targets = {"up": me + PLANE, "down": me - PLANE, "u": next_u, "v": next_v}
    slots = {"up": 0, "down": 1, "u": 2, "v": 3}

    load = pltpu.make_async_copy(
        stored.at[:, pl.ds(pl.multiple_of(grp * width, LANES), width)], rows.at[me], own_sem.at[0])
    load.start()
    mine = pltpu.make_async_copy(chunk.at[me], fac.at[grp, me], own_sem.at[1])
    load_ints = pltpu.make_async_copy(integrals, ints, own_sem.at[3])
    load_ints.start()
    load_virt = pltpu.make_async_copy(virtual, virt, own_sem.at[4])
    load_virt.start()
    pairs = pairs_in.at[0]
    nocc, nblocks, blk = occ.shape
    local = virtual.shape[1] // n_aux

    barrier = pltpu.get_barrier_semaphore()
    for o in range(1, n_aux):
        pl.semaphore_signal(barrier, inc=1, device_id=(lax.rem(me + o, n_aux), grp), device_id_type=MESH)
    for o in range(1, n_grp):
        pl.semaphore_signal(barrier, inc=1, device_id=(me, lax.rem(grp + o, n_grp)), device_id_type=MESH)
    pl.semaphore_wait(barrier, n_aux - 1 + n_grp - 1)

    def copy(source, colour, way):
        at = rows.at[source, :, pl.ds(*spans[colour][:2])]
        return pltpu.make_async_remote_copy(
            src_ref=at, dst_ref=at,
            send_sem=send.at[colour, slots[way], source], recv_sem=recv.at[colour, source],
            device_id=(targets[way], grp), device_id_type=MESH)

    def when(condition, action):
        if condition is None:
            action()
        else:
            pl.when(condition)(action)

    edges = {"up": up, "down": down, "u": None, "v": None}

    def ways_of(dz, du, dv, colour):
        if dv:
            return ()
        along = ("up", "down") if dz == 0 else (("up",) if dz > 0 else ("down",))
        if colour == 0:
            return ("v",) if du else along + ("u", "v")
        if dz == 0 and du == 0:
            return ("u",) + along + ("v",)
        return along + ("v",)

    def source_of(dz, du, dv):
        return (z - dz) * PLANE + su * (u + du * (1 - 2 * u)) + sv * (v + dv * (1 - 2 * v))

    def valid(dz):
        if dz == 0:
            return None
        return z - dz >= 0 if dz > 0 else z - dz < line

    sent = []

    def forward(dz, du, dv):
        source = source_of(dz, du, dv)
        for colour in range(len(spans)):
            ways = ways_of(dz, du, dv, spans[colour][2])
            sent.append((dz, source, colour, ways))

            def act(colour=colour, ways=ways):
                if (dz, du, dv) != (0, 0, 0):
                    copy(source, colour, "v").wait_recv()
                for way in ways:
                    when(edges[way], copy(source, colour, way).start)

            when(valid(dz), act)

    def plane_dot(dz, first):
        def act():
            base = (z - dz) * PLANE
            tile = 512 if width % 512 == 0 else LANES

            @pl.loop(0, width // tile)
            def _(t):
                cols = pl.ds(pl.multiple_of(t * tile, tile), tile)
                right = rows[pl.ds(base, PLANE), :, cols].reshape(-1, tile)
                for q in range(n_grp):
                    left = fac[q, pl.ds(base, PLANE)].reshape(-1, fac.shape[3])
                    term = lax.dot_general(
                        left, right, (((0,), (0,)), ((), ())), preferred_element_type=jnp.float32)
                    if first:
                        total[q, :, cols] = term
                    else:
                        total[q, :, cols] += term

        when(valid(dz), act)

    offsets = [(dz, du, dv) for dz in range(1 - line, line) for du in (0, 1) for dv in (0, 1)]
    hops = lambda o: abs(o[0]) + o[1] + o[2]
    last_hop = line + 1

    def fac_copy(o):
        to = lax.rem(me + o, n_aux)
        return pltpu.make_async_remote_copy(
            src_ref=chunk.at[to], dst_ref=fac.at[grp, me], send_sem=fsend.at[o], recv_sem=frecv.at[o],
            device_id=(to, grp), device_id_type=MESH)

    def fac_wait(o):
        source = lax.rem(me + n_aux - o, n_aux)
        pltpu.make_async_remote_copy(
            src_ref=chunk.at[0], dst_ref=fac.at[grp, source], send_sem=fsend.at[o], recv_sem=frecv.at[o],
            device_id=(source, grp), device_id_type=MESH).wait_recv()
        return source

    def share(o, source, p):
        return pltpu.make_async_remote_copy(
            src_ref=fac.at[grp, source], dst_ref=fac.at[grp, source],
            send_sem=psend.at[p, o], recv_sem=precv.at[p, o],
            device_id=(me, lax.rem(grp + p, n_grp)), device_id_type=MESH)

    def half_copy(p):
        return pltpu.make_async_remote_copy(
            src_ref=half.at[grp], dst_ref=half.at[grp], send_sem=hsend.at[p], recv_sem=hrecv.at[p],
            device_id=(me, lax.rem(grp + p, n_grp)), device_id_type=MESH)

    for hop in range(last_hop + 1):
        if hop == 0:
            load.wait()
        for offset in offsets:
            if hops(offset) == hop:
                forward(*offset)
        if hop == 0:
            weigh(pairs, occ, weights)
            load_ints.wait()
            contract(blk, ints, weights, part)
            place(blk, pairs, part, turned, half, grp)
            for p in range(1, n_grp):
                half_copy(p).start()
        if hop == 1:
            for p in range(1, n_grp):
                giver = lax.rem(grp + n_grp - p, n_grp)
                pltpu.make_async_remote_copy(
                    src_ref=half.at[giver], dst_ref=half.at[giver], send_sem=hsend.at[p],
                    recv_sem=hrecv.at[p], device_id=(me, giver), device_id_type=MESH).wait_recv()
            load_virt.wait()
            multiply(nocc, local, half, virt, chunk)
            mine.start()
            for o in range(1, n_aux):
                fac_copy(o).start()
            mine.wait()
        if hop == 2:
            for o in range(n_aux):
                source = me if o == 0 else fac_wait(o)
                for p in range(1, n_grp):
                    share(o, source, p).start()
            for o in range(n_aux):
                source = lax.rem(me + n_aux - o, n_aux)
                for p in range(1, n_grp):
                    giver = lax.rem(grp + n_grp - p, n_grp)
                    pltpu.make_async_remote_copy(
                        src_ref=fac.at[grp, source], dst_ref=fac.at[giver, source],
                        send_sem=psend.at[p, o], recv_sem=precv.at[p, o],
                        device_id=(me, giver), device_id_type=MESH).wait_recv()
        if hop >= 2:
            for dz in sorted({hop - 2, 2 - hop}):
                plane_dot(dz, hop == 2)

    def give(p, n):
        to = lax.rem(grp + p, n_grp)
        cols = pl.ds(*spans[n][:2])
        return pltpu.make_async_remote_copy(
            src_ref=block.at[to, :, cols], dst_ref=out.at[grp, :, cols],
            send_sem=osend.at[p, n], recv_sem=orecv.at[p, n],
            device_id=(me, to), device_id_type=MESH)

    for p in range(1, n_grp):
        to = lax.rem(grp + p, n_grp)
        for n in range(len(spans)):
            cols = pl.ds(*spans[n][:2])
            block[to, :, cols] = total[to, :, cols].astype(block.dtype)
            give(p, n).start()
    block[grp] = total[grp].astype(block.dtype)
    keep = pltpu.make_async_copy(block.at[grp], out.at[grp], own_sem.at[2])
    keep.start()

    for dz, source, colour, ways in sent:
        def drain(source=source, colour=colour, ways=ways):
            for way in ways:
                when(edges[way], copy(source, colour, way).wait_send)
        if ways:
            when(valid(dz), drain)
    for p in range(1, n_grp):
        half_copy(p).wait_send()
    for o in range(1, n_aux):
        fac_copy(o).wait_send()
    for o in range(n_aux):
        source = lax.rem(me + n_aux - o, n_aux)
        for p in range(1, n_grp):
            share(o, source, p).wait_send()
    for p in range(1, n_grp):
        giver = lax.rem(grp + n_grp - p, n_grp)
        for n in range(len(spans)):
            cols = pl.ds(*spans[n][:2])
            give(p, n).wait_send()
            pltpu.make_async_remote_copy(
                src_ref=block.at[giver, :, cols], dst_ref=out.at[giver, :, cols],
                send_sem=osend.at[p, n], recv_sem=orecv.at[p, n],
                device_id=(me, giver), device_id_type=MESH).wait_recv()
    keep.wait()


def panels_any(integrals, pairs, occ, virtual, stored, n_aux, n_grp):
    depth = stored.shape[0]
    width = stored.shape[1] // n_grp
    aux_rows, nb, flat = integrals.shape
    nocc, nblocks, blk = occ.shape
    nbas, slab = virtual.shape
    pieces = len(spans_of(width))
    cols = nocc * (slab // n_aux)
    dma = pltpu.SemaphoreType.DMA
    hbm = pl.BlockSpec(memory_space=pltpu.HBM)
    vmem = pl.BlockSpec(memory_space=pltpu.VMEM)
    return pl.pallas_call(
        functools.partial(panel_any_kernel, n_aux, n_grp),
        out_shape=jax.ShapeDtypeStruct((n_grp, cols, width), jnp.bfloat16),
        in_specs=[hbm, vmem, vmem, hbm, hbm],
        out_specs=hbm,
        scratch_shapes=[
            pltpu.VMEM((n_aux, depth, width), jnp.bfloat16),
            pltpu.VMEM((n_grp, n_aux, depth, cols), jnp.bfloat16),
            pltpu.VMEM((n_grp, cols, width), jnp.float32),
            pltpu.VMEM((n_grp, cols, width), jnp.bfloat16),
            pltpu.VMEM(integrals.shape, jnp.bfloat16),
            pltpu.VMEM(virtual.shape, jnp.bfloat16),
            pltpu.VMEM((nocc, nb, flat), jnp.float32),
            pltpu.VMEM((nocc * aux_rows, nb, LANES), jnp.float32),
            pltpu.VMEM((nb, nocc * aux_rows, LANES), jnp.float32),
            pltpu.VMEM((n_grp, nocc * aux_rows, nbas), jnp.bfloat16),
            pltpu.VMEM((n_aux, depth, cols), jnp.bfloat16),
            dma((5,)),
            dma((pieces, n_aux)),
            dma((pieces, 4, n_aux)),
            dma((n_aux,)),
            dma((n_aux,)),
            dma((n_grp, n_aux)),
            dma((n_grp, n_aux)),
            dma((n_grp, pieces)),
            dma((n_grp, pieces)),
            dma((n_grp,)),
            dma((n_grp,)),
        ],
        compiler_params=pltpu.CompilerParams(
            collective_id=0, has_side_effects=True, vmem_limit_bytes=63 * 1024 * 1024),
    )(integrals, pairs, occ, virtual, stored)


HALVE, OWN, OTHER, FACTOR, CROSS, TURN, STORED, FINISH = range(8)
JOINT = 0.67
TUNED = (
    (6, 1, 0, 0), (6, 3, 0, 0), (0,), (6, 5, 0, 0), (6, 1, 1, 0), (6, 0, 0, 0), (6, 2, 0, 1), (6, 3, 1, 0), (1,),
    (6, 1, 2, 0), (6, 1, 0, 1), (6, 5, 0, 1), (6, 2, 0, 0), (6, 3, 0, 1), (6, 1, 3, 0), (6, 3, 2, 0), (2,),
    (6, 2, 1, 0), (6, 5, 1, 1), (6, 1, 1, 1), (6, 3, 3, 0), (3, 0), (3, 2), (3, 3), (3, 5), (3, 4), (6, 3, 1, 1),
    (4, 0), (6, 2, 2, 0), (3, 6), (4, 3), (6, 2, 3, 0), (6, 5, 1, 0), (3, 1), (3, 7), (6, 0, 0, 1), (4, 2),
    (6, 1, 2, 1), (6, 2, 1, 1), (6, 1, 3, 1), (6, 5, 2, 0), (6, 3, 2, 1), (6, 5, 2, 1), (6, 4, 0, 0), (4, 5), (4, 1),
    (6, 2, 2, 1), (6, 5, 3, 0), (4, 6), (4, 4), (6, 3, 3, 1), (6, 0, 1, 0), (6, 0, 1, 1), (6, 4, 0, 1), (4, 7),
    (6, 5, 3, 1), (5,), (7, 1), (6, 0, 2, 0), (6, 0, 2, 1), (6, 4, 1, 1), (6, 0, 3, 0), (7, 3), (6, 2, 3, 1),
    (6, 4, 1, 0), (6, 0, 3, 1), (6, 4, 2, 1), (7, 5), (7, 2), (6, 4, 2, 0), (6, 4, 3, 0), (6, 4, 3, 1), (7, 0),
    (7, 4),
)


def plan(pieces, line, n_pairs):
    stored = [(STORED, n, hop, far) for hop in range(line) for far in (0, 1) for n in range(pieces + 2)]
    factor = [(kind, o) for kind in (FACTOR, CROSS) for o in range(n_pairs)]
    plain = [(HALVE,), (OWN,), (OTHER,)] + stored + factor + [(TURN,)] + [(FINISH, n) for n in range(pieces + 2)]
    return TUNED if sorted(TUNED) == sorted(plain) else plain


def weigh_blocks(pairs, occ, weights):
    nocc, nbas = occ.shape
    nb = pairs.shape[1]
    blk = math.isqrt(weights.shape[2])
    per = LANES // blk
    tiles = nbas // LANES
    line = lax.broadcasted_iota(jnp.int32, (tiles, nb), 0) * per
    step = 8 * LANES
    row = lax.broadcasted_iota(jnp.int32, (blk, step), 0) * blk
    col = lax.broadcasted_iota(jnp.int32, (blk, step), 1)
    orbital = occ[...].astype(jnp.float32)
    for i in range(nocc):
        table = jnp.concatenate(
            [orbital[i:i + 1, t * LANES:(t + 1) * LANES] for t in range(tiles)], axis=0).astype(jnp.bfloat16)
        picked = None
        for f in range(per):
            pick = (pairs[0:1, :] == line + f).astype(jnp.bfloat16)
            term = lax.dot_general(
                pick, table[:, f * blk:(f + 1) * blk], (((0,), (0,)), ((), ())), preferred_element_type=jnp.float32)
            picked = term if picked is None else picked + term
        picked = picked.astype(jnp.bfloat16)
        for t in range(weights.shape[2] // step):
            offset = col + t * step - row
            spread = ((offset >= 0) & (offset < blk)).astype(jnp.bfloat16)
            weights[i, :, t * step:(t + 1) * step] = jnp.dot(
                picked, spread, preferred_element_type=jnp.float32)


def compact(blk, part, half, grp):
    nb = part.shape[1]
    per = LANES // blk
    lane = lax.broadcasted_iota(jnp.int32, (part.shape[0], LANES), 1) // blk
    for t in range(nb // per):
        tile = part[:, t * per, :]
        for f in range(1, per):
            tile = jnp.where(lane == f, part[:, t * per + f, :], tile)
        half[grp, :, t * LANES:(t + 1) * LANES] = tile.astype(half.dtype)


def expand(nocc, local, q, index, half, virt, chunk):
    n_grp, both, depth = half.shape
    blk = virt.shape[1]
    aux_rows = both // nocc
    wide = 2 * local
    step = math.lcm(wide, 2 * LANES)
    top = pl.ds(pl.multiple_of(q * aux_rows, aux_rows), aux_rows)
    for t in range(virt.shape[2] // step):
        cols = slice(t * step, (t + 1) * step)
        right = jnp.concatenate([virt[index[q, 1, k], :, cols] for k in range(depth // blk)], axis=0)
        product = jnp.dot(half[q], right, preferred_element_type=jnp.float32).astype(chunk.dtype)
        for c in range(step // wide):
            for i in range(nocc):
                chunk[t * (step // wide) + c, top, i * wide:(i + 1) * wide] = product[
                    i * aux_rows:(i + 1) * aux_rows, c * wide:(c + 1) * wide]


def panel_kernel(n_aux, v, integrals, pairs_in, occ_in, virtual, stored, out, rows, wides, fac, turned, block, slab,
                 ints, virt, weights, part, half, chunk, pairs, index, occ,
                 load_sem, own_sem, xsend, xrecv, send, recv, own_wide, xsend_wide, xrecv_wide, send_wide, recv_wide,
                 hsend, hrecv, fsend, frecv, gsend, grecv, psend, precv, osend, orecv, wsend, wrecv):
    me = lax.axis_index("aux")
    grp = lax.axis_index("grp")
    other = 1 - grp
    line = n_aux // PLANE
    nj = stored.shape[1] // v
    pieces = rows.shape[0]
    piece = rows.shape[3] // nj
    wide = wides.shape[3] // nj
    base = 4 * pieces * piece
    nocc = occ.shape[0]
    blk = virtual.shape[1]
    local = virtual.shape[2] // n_aux
    z = me // PLANE
    x = me % 2
    y = (me // 2) % 2
    pair = me // 2
    n_pairs = n_aux // 2
    xmate = me + 1 - 2 * x
    ymate = me + 2 * (1 - 2 * y)
    edges = {"up": z + 1 < line, "down": z >= 1, "x": None, "y": None}
    targets = {"up": me + PLANE, "down": me - PLANE, "x": xmate, "y": ymate}
    slots = {"up": 0, "down": 1, "x": 2, "y": 2}
    mine = 2 * x + grp
    theirs = 2 * (1 - x) + grp

    def column(j, q, n):
        return pl.ds(pl.multiple_of(j * v + (q * pieces + n) * piece, LANES), piece)

    def column_wide(j, core, n):
        return pl.ds(pl.multiple_of(j * v + base + (core * 2 + n) * wide, LANES), wide)

    narrow = dict(
        ref=rows, width=piece, own=own_sem, xsend=xsend, xrecv=xrecv, send=send, recv=recv, mate=xmate, last="y",
        here=lambda j, n: column(j, mine, n), there=lambda j, n: column(j, theirs, n))
    broad = [dict(
        ref=wides, width=wide, own=own_wide, xsend=xsend_wide, xrecv=xrecv_wide, send=send_wide, recv=recv_wide,
        mate=mate, last=last, here=lambda j, n: column_wide(j, grp, n), there=lambda j, n: column_wide(j, grp, n))
        for mate, last in ((xmate, "y"), (ymate, "x"))]
    every = [(narrow, n) for n in range(pieces)] + [(broad[n], n) for n in range(2)]

    def at_of(kind, n, source, j):
        return kind["ref"].at[n, source, :, pl.ds(j * kind["width"], kind["width"])]

    def own_copy(kind, n, j):
        return pltpu.make_async_copy(stored.at[:, kind["here"](j, n)], at_of(kind, n, me, j), kind["own"].at[n, j])

    load_pairs = pltpu.make_async_copy(pairs_in.at[0], pairs.at[grp], load_sem.at[0])
    load_pairs.start()
    load_occ = pltpu.make_async_copy(occ_in, occ, load_sem.at[1])
    load_occ.start()
    load_index = pltpu.make_async_copy(pairs_in.at[0], index.at[grp], load_sem.at[4])
    load_index.start()
    load_ints = pltpu.make_async_copy(integrals, ints, load_sem.at[2])
    load_ints.start()
    for kind, n in every:
        for j in range(nj):
            own_copy(kind, n, j).start()
    load_virt = pltpu.make_async_copy(virtual, virt, load_sem.at[3])
    load_virt.start()

    barrier = pltpu.get_barrier_semaphore()
    peers = [((pair + o) % n_pairs * 2 + x, grp) for o in range(1, n_pairs)]
    peers += [(xmate, grp), (xmate, other), (me, other)]
    for peer in peers:
        pl.semaphore_signal(barrier, inc=1, device_id=peer, device_id_type=MESH)

    def when(condition, action):
        if condition is None:
            action()
        else:
            pl.when(condition)(action)

    def remote(src, dst, send_sem, recv_sem, device):
        return pltpu.make_async_remote_copy(
            src_ref=src, dst_ref=dst, send_sem=send_sem, recv_sem=recv_sem, device_id=device, device_id_type=MESH)

    def copy(kind, n, source, way):
        at = kind["ref"].at[n, source]
        return remote(
            at, at, kind["send"].at[n, slots[way], source], kind["recv"].at[n, source], (targets[way], grp))

    def cross(kind, n, j):
        return remote(
            stored.at[:, kind["there"](j, n)], at_of(kind, n, me, j),
            kind["xsend"].at[n, j], kind["xrecv"].at[n, j], (kind["mate"], grp))

    def cross_wait(kind, n, j):
        at = at_of(kind, n, kind["mate"], j)
        remote(at, at, kind["xsend"].at[n, j], kind["xrecv"].at[n, j], (kind["mate"], grp)).wait_recv()

    def valid(dz):
        if dz == 0:
            return None
        return z - dz >= 0 if dz > 0 else z - dz < line

    sent = []

    def forward(kind, n, dz, far):
        source = (kind["mate"] if far else me) - dz * PLANE
        last = kind["last"]
        ways = ("up", "down", last) if dz == 0 else (("up", last) if dz > 0 else ("down", last))
        sent.append((kind, n, dz, source, ways))

        def act():
            if dz == 0:
                for j in range(nj):
                    if far:
                        cross_wait(kind, n, j)
                    else:
                        own_copy(kind, n, j).wait()
            else:
                copy(kind, n, source, last).wait_recv()
            for way in ways:
                when(edges[way], copy(kind, n, source, way).start)

        when(valid(dz), act)

    def stage(group, distance, *fars):
        for kind, n in group:
            for far in fars:
                for dz in sorted({distance, -distance}):
                    forward(kind, n, dz, far)

    def half_copy():
        return remote(half.at[grp], half.at[grp], hsend.at[0], hrecv.at[0], (me, other))

    def pairs_copy():
        return remote(pairs.at[grp], pairs.at[grp], hsend.at[1], hrecv.at[1], (me, other))

    def fac_copy(o):
        to = (pair + o) % n_pairs
        return remote(chunk.at[to], fac.at[grp, me], fsend.at[o], frecv.at[o], (to * 2 + x, grp))

    def fac_source(o):
        return (pair + n_pairs - o) % n_pairs * 2

    def fac_cross(o):
        source = fac_source(o) + x
        return remote(fac.at[grp, source], fac.at[grp, source], gsend.at[o], grecv.at[o], (xmate, grp))

    def share(o, far):
        source = fac_source(o) + (1 - x if far else x)
        return remote(
            fac.at[grp, source], fac.at[grp, source], psend.at[int(far), o], precv.at[int(far), o], (me, other))

    def give(n, rel, q, j):
        to = (grp + q) % 2
        chip = 1 - x if rel else x
        src = block.at[n, to, chip]
        dst = out.at[:, :, column(0, mine, n)]
        if not rel and not q:
            return pltpu.make_async_copy(src, dst, osend.at[n, 0, j])
        return remote(
            src, dst, osend.at[n, 2 * rel + q, j], orecv.at[n, 2 * rel + q, j], (xmate if rel else me, to))

    def taken(n, rel, q, j):
        source = 2 * (1 - x if rel else x) + (grp + q) % 2
        return remote(
            block.at[n, 0, 0], out.at[:, :, column(0, source, n)],
            osend.at[n, 2 * rel + q, j], orecv.at[n, 2 * rel + q, j], (xmate, grp))

    def pass_over(n, q, j):
        to = (grp + q) % 2
        src = slab.at[n, to]
        dst = out.at[:, :, column_wide(0, grp, n)]
        if not q:
            return pltpu.make_async_copy(src, dst, wsend.at[n, q, j])
        return remote(src, dst, wsend.at[n, q, j], wrecv.at[n, j], (me, to))

    def passed(n, j):
        return remote(
            slab.at[n, 0], out.at[:, :, column_wide(0, other, n)],
            wsend.at[n, 1, j], wrecv.at[n, j], (me, other))

    def arrivals(kind, n):
        mate = ymate if kind["last"] == "y" else xmate
        for dz in range(1 - line, line):
            for far in (0, 1):
                step = (kind["mate"] - me) if far else 0

                def arrive(source=mate + step - dz * PLANE):
                    copy(kind, n, source, kind["last"]).wait_recv()

                when(valid(dz), arrive)

    def finish(n):
        arrivals(narrow, n)
        right = rows[n].reshape(-1, nj * piece)
        for q in range(2):
            left = turned[q].reshape(-1, right.shape[0])
            term = jnp.dot(left, right, preferred_element_type=jnp.float32).astype(block.dtype)
            for chip in range(2):
                for j in range(nj):
                    block[n, q, chip, :, j, :] = term[
                        chip * nocc * local:(chip + 1) * nocc * local, j * piece:(j + 1) * piece]
        for rel, q in ((1, 0), (1, 1), (0, 1), (0, 0)):
            give(n, rel, q, 0).start()

    def finish_wide(n):
        arrivals(broad[n], n)
        tile = math.gcd(2 * LANES, wide)
        for q in (1, 0):
            to = (grp + q) % 2
            for t in range(nj * wide // tile):
                cols = slice(t * tile, (t + 1) * tile)
                right = wides[n, :, :, cols].reshape(-1, tile)
                j, start = t * tile // wide, t * tile % wide
                slab[n, to, :, j, start:start + tile] = jnp.dot(
                    turned[to, x], right, preferred_element_type=jnp.float32).astype(slab.dtype)
            pass_over(n, q, 0).start()

    def wait_fac(o):
        if o:
            source = fac_source(o) + x
            remote(fac.at[grp, source], fac.at[grp, source], fsend.at[o], frecv.at[o], (source, grp)).wait_recv()
        else:
            keep.wait()
        fac_cross(o).start()
        share(o, False).start()

    def wait_cross(o):
        source = fac_source(o) + 1 - x
        remote(fac.at[grp, source], fac.at[grp, source], gsend.at[o], grecv.at[o], (xmate, grp)).wait_recv()
        share(o, True).start()

    def halve():
        compact(blk, part, half, grp)
        half_copy().start()

    def expand_own():
        load_index.wait()
        load_virt.wait()
        expand(nocc, local, grp, index, half, virt, chunk)

    def expand_other():
        remote(pairs.at[other], pairs.at[other], hsend.at[1], hrecv.at[1], (me, other)).wait_recv()
        load_other = pltpu.make_async_copy(pairs.at[other], index.at[other], load_sem.at[0])
        load_other.start()
        load_other.wait()
        remote(half.at[other], half.at[other], hsend.at[0], hrecv.at[0], (me, other)).wait_recv()
        expand(nocc, local, other, index, half, virt, chunk)
        for o in range(1, n_pairs):
            fac_copy(o).start()
        keep.start()

    def turn():
        for far in (False, True):
            for o in range(n_pairs):
                at = fac.at[other, fac_source(o) + (1 - x if far else x)]
                remote(at, at, psend.at[int(far), o], precv.at[int(far), o], (me, other)).wait_recv()
        group = LANES // fac.shape[2]
        for q in range(2):
            for t in range(n_aux // group):
                tall = fac[q, t * group:(t + 1) * group].reshape(LANES, -1).T
                for i in range(nocc):
                    for chip in range(2):
                        top = (i * 2 + chip) * local
                        turned[q, chip, i * local:(i + 1) * local, t * LANES:(t + 1) * LANES] = tall[top:top + local]

    keep = pltpu.make_async_copy(chunk.at[pair], fac.at[grp, me], load_sem.at[1])
    load_pairs.wait()
    load_occ.wait()
    weigh_blocks(pairs[grp], occ, weights)
    load_ints.wait()
    contract(blk, ints, weights, part)
    pl.semaphore_wait(barrier, len(peers))
    pairs_copy().start()
    for kind, n in every:
        for j in range(nj):
            cross(kind, n, j).start()
    steps = {
        HALVE: halve, OWN: expand_own, OTHER: expand_other, FACTOR: wait_fac, CROSS: wait_cross, TURN: turn,
        STORED: lambda n, hop, far: stage([every[n]], hop, far),
        FINISH: lambda n: finish(n) if n < pieces else finish_wide(n - pieces)}
    for step, *operands in plan(pieces, line, n_pairs):
        steps[step](*operands)

    for kind, n, dz, source, ways in sent:
        def drain(kind=kind, n=n, source=source, ways=ways):
            for way in ways:
                when(edges[way], copy(kind, n, source, way).wait_send)
        when(valid(dz), drain)
    for kind, n in every:
        for j in range(nj):
            cross(kind, n, j).wait_send()
    half_copy().wait_send()
    pairs_copy().wait_send()
    for o in range(n_pairs):
        if o:
            fac_copy(o).wait_send()
        fac_cross(o).wait_send()
        share(o, False).wait_send()
        share(o, True).wait_send()
    for n in range(pieces):
        for j in range(1):
            for rel, q in ((1, 0), (1, 1), (0, 1)):
                give(n, rel, q, j).wait_send()
                taken(n, rel, q, j).wait_recv()
            give(n, 0, 0, j).wait()
    for n in range(2):
        for j in range(1):
            pass_over(n, 1, j).wait_send()
            passed(n, j).wait_recv()
            pass_over(n, 0, j).wait()


def panels(integrals, pairs, occupied, virtual, stored, n_aux, v):
    depth = stored.shape[0]
    aux_rows, nb, flat = integrals.shape
    nocc = occupied.shape[0]
    blk = math.isqrt(flat)
    slab = virtual.shape[2]
    nj = stored.shape[1] // v
    piece = LANES
    pieces = round(v // (4 * piece) * JOINT)
    wide = (v - 4 * pieces * piece) // 4
    cols = nocc * (slab // n_aux)
    n_pairs = n_aux // 2
    dma = pltpu.SemaphoreType.DMA
    hbm = pl.BlockSpec(memory_space=pltpu.HBM)
    return pl.pallas_call(
        functools.partial(panel_kernel, n_aux, v),
        out_shape=jax.ShapeDtypeStruct((cols, nj, v), jnp.bfloat16),
        in_specs=[hbm] * 5,
        out_specs=hbm,
        scratch_shapes=[
            pltpu.VMEM((pieces, n_aux, depth, nj * piece), jnp.bfloat16),
            pltpu.VMEM((2, n_aux, depth, nj * wide), jnp.bfloat16),
            pltpu.VMEM((2, n_aux, depth, 2 * cols), jnp.bfloat16),
            pltpu.VMEM((2, 2, cols, n_aux * depth), jnp.bfloat16),
            pltpu.VMEM((pieces, 2, 2, cols, nj, piece), jnp.bfloat16),
            pltpu.VMEM((2, 2, cols, nj, wide), jnp.bfloat16),
            pltpu.VMEM(integrals.shape, jnp.bfloat16),
            pltpu.VMEM(virtual.shape, jnp.bfloat16),
            pltpu.VMEM((nocc, nb, flat), jnp.float32),
            pltpu.VMEM((nocc * aux_rows, nb, LANES), jnp.float32),
            pltpu.VMEM((2, nocc * aux_rows, nb * blk), jnp.bfloat16),
            pltpu.VMEM((n_pairs, depth, 2 * cols), jnp.bfloat16),
            pltpu.VMEM((2, 2, nb), jnp.int32),
            pltpu.SMEM((2, 2, nb), jnp.int32),
            pltpu.VMEM(occupied.shape, jnp.bfloat16),
            dma((5,)),
            dma((pieces, nj)),
            dma((pieces, nj)),
            dma((pieces, nj)),
            dma((pieces, 3, n_aux)),
            dma((pieces, n_aux)),
            dma((2, nj)),
            dma((2, nj)),
            dma((2, nj)),
            dma((2, 3, n_aux)),
            dma((2, n_aux)),
            dma((2,)),
            dma((2,)),
            dma((n_pairs,)),
            dma((n_pairs,)),
            dma((n_pairs,)),
            dma((n_pairs,)),
            dma((2, n_pairs)),
            dma((2, n_pairs)),
            dma((pieces, 4, nj)),
            dma((pieces, 4, nj)),
            dma((2, 2, nj)),
            dma((2, nj)),
        ],
        compiler_params=pltpu.CompilerParams(
            collective_id=0, has_side_effects=True, vmem_limit_bytes=63 * 1024 * 1024),
    )(integrals, pairs, occupied, virtual, stored)


def make_per_device(n_aux, n_grp, v):
    def per_device(integrals, block_pairs, occupied, virtual, stored):
        nocc, nbas = occupied.shape
        local = virtual.shape[1] // n_aux
        blk = math.isqrt(integrals.shape[2])
        if n_grp == 2 and n_aux % PLANE == 0 and v % (4 * LANES) == 0 and LANES % stored.shape[0] == 0:
            panel = panels(integrals, block_pairs.transpose(0, 2, 1), occupied,
                           virtual.reshape(nbas // blk, blk, -1), stored, n_aux, v)
            return panel.reshape(nocc, local, panel.shape[1], v)
        occ = occupied.reshape(nocc, nbas // blk, blk)
        panel = panels_any(integrals, block_pairs, occ, virtual, stored, n_aux, n_grp)
        return panel.transpose(1, 0, 2).reshape(nocc, local, n_grp * panel.shape[2] // v, v)

    return per_device


def solution(mesh):
    n_aux, n_grp = mesh.shape["aux"], mesh.shape["grp"]

    def whole(integrals, block_pairs, occupied, virtual, stored):
        return jax.shard_map(
            make_per_device(n_aux, n_grp, virtual.shape[1]),
            mesh=mesh,
            in_specs=(
                P(("aux", "grp"), None, None),
                P(("aux", "grp"), None, None),
                P(),
                P(None, "grp"),
                P("aux", None),
            ),
            out_specs=P(None, ("grp", "aux"), None, None),
            check_vma=False,
        )(integrals, block_pairs, occupied, virtual, stored)

    return whole
```

```python
import functools
import math

import jax
import jax.numpy as jnp
from jax import lax
from jax.experimental import pallas as pl
from jax.experimental.pallas import tpu as pltpu
from jax.sharding import PartitionSpec as P

MESH = pl.DeviceIdType.MESH
LANES = 128
PLANE = 4
PIECES = 3
FIRST = 1


def spans_of(width):
    piece = width // PIECES // LANES * LANES
    starts = [n * piece for n in range(PIECES)] + [width]
    return [(a, b - a, 0 if n < FIRST else 1) for n, (a, b) in enumerate(zip(starts, starts[1:]))]


def weigh(pairs, occ, weights):
    nb = pairs.shape[0]
    nocc, nblocks, blk = occ.shape
    lanes = lax.broadcasted_iota(jnp.int32, (nb, nblocks), 1)
    pick = (pairs[:, 0:1] == lanes).astype(jnp.bfloat16)
    step = 8 * LANES
    row = lax.broadcasted_iota(jnp.int32, (blk, step), 0) * blk
    col = lax.broadcasted_iota(jnp.int32, (blk, step), 1)
    for i in range(nocc):
        picked = jnp.dot(pick, occ[i], preferred_element_type=jnp.float32).astype(jnp.bfloat16)
        for t in range(weights.shape[2] // step):
            offset = col + t * step - row
            spread = ((offset >= 0) & (offset < blk)).astype(jnp.bfloat16)
            weights[i, :, t * step:(t + 1) * step] = jnp.dot(
                picked, spread, preferred_element_type=jnp.float32)


def contract(blk, integrals, weights, part):
    aux_rows = integrals.shape[0]
    nocc = weights.shape[0]

    @pl.loop(0, aux_rows)
    def _(p):
        for i in range(nocc):
            sums = [None, None]
            for t in range(integrals.shape[2] // LANES):
                cols = slice(t * LANES, (t + 1) * LANES)
                term = integrals[p, :, cols].astype(jnp.float32) * weights[i, :, cols]
                sums[t % 2] = term if sums[t % 2] is None else sums[t % 2] + term
            total = sums[0] + sums[1]
            whole = total
            for f in range(1, LANES // blk):
                whole = whole + pltpu.roll(total, f * blk, 1)
            part[i * aux_rows + p] = whole


def place(blk, pairs, part, turned, half, grp):
    nb = pairs.shape[0]
    per = LANES // blk
    for k in range(nb):
        turned[k] = part[:, k, :]
    lane = lax.broadcasted_iota(jnp.int32, (1, LANES), 1) // blk

    @pl.loop(0, half.shape[2] // LANES)
    def _(b):
        here = lane + b * per
        total = None
        for k in range(nb):
            term = jnp.where(here == pairs[k:k + 1, 1:2], turned[k], 0.0)
            total = term if total is None else total + term
        half[grp, :, pl.ds(pl.multiple_of(b * LANES, LANES), LANES)] = total.astype(half.dtype)


def multiply(nocc, local, half, virt, chunk):
    n_grp, both, nbas = half.shape
    aux_rows = both // nocc
    step = math.lcm(local, LANES)
    for t in range(virt.shape[1] // step):
        product = jnp.dot(
            half[...].reshape(n_grp * both, nbas), virt[:, t * step:(t + 1) * step],
            preferred_element_type=jnp.float32)
        for c in range(step // local):
            d = t * (step // local) + c
            for q in range(n_grp):
                for i in range(nocc):
                    top = q * both + i * aux_rows
                    chunk[d, q * aux_rows:(q + 1) * aux_rows, i * local:(i + 1) * local] = product[
                        top:top + aux_rows, c * local:(c + 1) * local].astype(chunk.dtype)


def panel_any_kernel(n_aux, n_grp, integrals, pairs_in, occ, virtual, stored, out, rows, fac, total, block,
                 ints, virt, weights, part, turned, half, chunk,
                 own_sem, recv, send, frecv, fsend, precv, psend, orecv, osend, hrecv, hsend):
    me = lax.axis_index("aux")
    grp = lax.axis_index("grp")
    line = n_aux // PLANE
    width = rows.shape[2]
    spans = spans_of(width)
    z = me // PLANE
    su = 1 + grp % 2
    sv = 3 - su
    u = (me // su) % 2
    v = (me // sv) % 2
    next_u = me + su * (1 - 2 * u)
    next_v = me + sv * (1 - 2 * v)
    up, down = z + 1 < line, z >= 1
    targets = {"up": me + PLANE, "down": me - PLANE, "u": next_u, "v": next_v}
    slots = {"up": 0, "down": 1, "u": 2, "v": 3}

    load = pltpu.make_async_copy(
        stored.at[:, pl.ds(pl.multiple_of(grp * width, LANES), width)], rows.at[me], own_sem.at[0])
    load.start()
    mine = pltpu.make_async_copy(chunk.at[me], fac.at[grp, me], own_sem.at[1])
    load_ints = pltpu.make_async_copy(integrals, ints, own_sem.at[3])
    load_ints.start()
    load_virt = pltpu.make_async_copy(virtual, virt, own_sem.at[4])
    load_virt.start()
    pairs = pairs_in.at[0]
    nocc, nblocks, blk = occ.shape
    local = virtual.shape[1] // n_aux

    barrier = pltpu.get_barrier_semaphore()
    for o in range(1, n_aux):
        pl.semaphore_signal(barrier, inc=1, device_id=(lax.rem(me + o, n_aux), grp), device_id_type=MESH)
    for o in range(1, n_grp):
        pl.semaphore_signal(barrier, inc=1, device_id=(me, lax.rem(grp + o, n_grp)), device_id_type=MESH)
    pl.semaphore_wait(barrier, n_aux - 1 + n_grp - 1)

    def copy(source, colour, way):
        at = rows.at[source, :, pl.ds(*spans[colour][:2])]
        return pltpu.make_async_remote_copy(
            src_ref=at, dst_ref=at,
            send_sem=send.at[colour, slots[way], source], recv_sem=recv.at[colour, source],
            device_id=(targets[way], grp), device_id_type=MESH)

    def when(condition, action):
        if condition is None:
            action()
        else:
            pl.when(condition)(action)

    edges = {"up": up, "down": down, "u": None, "v": None}

    def ways_of(dz, du, dv, colour):
        if dv:
            return ()
        along = ("up", "down") if dz == 0 else (("up",) if dz > 0 else ("down",))
        if colour == 0:
            return ("v",) if du else along + ("u", "v")
        if dz == 0 and du == 0:
            return ("u",) + along + ("v",)
        return along + ("v",)

    def source_of(dz, du, dv):
        return (z - dz) * PLANE + su * (u + du * (1 - 2 * u)) + sv * (v + dv * (1 - 2 * v))

    def valid(dz):
        if dz == 0:
            return None
        return z - dz >= 0 if dz > 0 else z - dz < line

    sent = []

    def forward(dz, du, dv):
        source = source_of(dz, du, dv)
        for colour in range(len(spans)):
            ways = ways_of(dz, du, dv, spans[colour][2])
            sent.append((dz, source, colour, ways))

            def act(colour=colour, ways=ways):
                if (dz, du, dv) != (0, 0, 0):
                    copy(source, colour, "v").wait_recv()
                for way in ways:
                    when(edges[way], copy(source, colour, way).start)

            when(valid(dz), act)

    def plane_dot(dz, first):
        def act():
            base = (z - dz) * PLANE
            tile = 512 if width % 512 == 0 else LANES

            @pl.loop(0, width // tile)
            def _(t):
                cols = pl.ds(pl.multiple_of(t * tile, tile), tile)
                right = rows[pl.ds(base, PLANE), :, cols].reshape(-1, tile)
                for q in range(n_grp):
                    left = fac[q, pl.ds(base, PLANE)].reshape(-1, fac.shape[3])
                    term = lax.dot_general(
                        left, right, (((0,), (0,)), ((), ())), preferred_element_type=jnp.float32)
                    if first:
                        total[q, :, cols] = term
                    else:
                        total[q, :, cols] += term

        when(valid(dz), act)

    offsets = [(dz, du, dv) for dz in range(1 - line, line) for du in (0, 1) for dv in (0, 1)]
    hops = lambda o: abs(o[0]) + o[1] + o[2]
    last_hop = line + 1

    def fac_copy(o):
        to = lax.rem(me + o, n_aux)
        return pltpu.make_async_remote_copy(
            src_ref=chunk.at[to], dst_ref=fac.at[grp, me], send_sem=fsend.at[o], recv_sem=frecv.at[o],
            device_id=(to, grp), device_id_type=MESH)

    def fac_wait(o):
        source = lax.rem(me + n_aux - o, n_aux)
        pltpu.make_async_remote_copy(
            src_ref=chunk.at[0], dst_ref=fac.at[grp, source], send_sem=fsend.at[o], recv_sem=frecv.at[o],
            device_id=(source, grp), device_id_type=MESH).wait_recv()
        return source

    def share(o, source, p):
        return pltpu.make_async_remote_copy(
            src_ref=fac.at[grp, source], dst_ref=fac.at[grp, source],
            send_sem=psend.at[p, o], recv_sem=precv.at[p, o],
            device_id=(me, lax.rem(grp + p, n_grp)), device_id_type=MESH)

    def half_copy(p):
        return pltpu.make_async_remote_copy(
            src_ref=half.at[grp], dst_ref=half.at[grp], send_sem=hsend.at[p], recv_sem=hrecv.at[p],
            device_id=(me, lax.rem(grp + p, n_grp)), device_id_type=MESH)

    for hop in range(last_hop + 1):
        if hop == 0:
            load.wait()
        for offset in offsets:
            if hops(offset) == hop:
                forward(*offset)
        if hop == 0:
            weigh(pairs, occ, weights)
            load_ints.wait()
            contract(blk, ints, weights, part)
            place(blk, pairs, part, turned, half, grp)
            for p in range(1, n_grp):
                half_copy(p).start()
        if hop == 1:
            for p in range(1, n_grp):
                giver = lax.rem(grp + n_grp - p, n_grp)
                pltpu.make_async_remote_copy(
                    src_ref=half.at[giver], dst_ref=half.at[giver], send_sem=hsend.at[p],
                    recv_sem=hrecv.at[p], device_id=(me, giver), device_id_type=MESH).wait_recv()
            load_virt.wait()
            multiply(nocc, local, half, virt, chunk)
            mine.start()
            for o in range(1, n_aux):
                fac_copy(o).start()
            mine.wait()
        if hop == 2:
            for o in range(n_aux):
                source = me if o == 0 else fac_wait(o)
                for p in range(1, n_grp):
                    share(o, source, p).start()
            for o in range(n_aux):
                source = lax.rem(me + n_aux - o, n_aux)
                for p in range(1, n_grp):
                    giver = lax.rem(grp + n_grp - p, n_grp)
                    pltpu.make_async_remote_copy(
                        src_ref=fac.at[grp, source], dst_ref=fac.at[giver, source],
                        send_sem=psend.at[p, o], recv_sem=precv.at[p, o],
                        device_id=(me, giver), device_id_type=MESH).wait_recv()
        if hop >= 2:
            for dz in sorted({hop - 2, 2 - hop}):
                plane_dot(dz, hop == 2)

    def give(p, n):
        to = lax.rem(grp + p, n_grp)
        cols = pl.ds(*spans[n][:2])
        return pltpu.make_async_remote_copy(
            src_ref=block.at[to, :, cols], dst_ref=out.at[grp, :, cols],
            send_sem=osend.at[p, n], recv_sem=orecv.at[p, n],
            device_id=(me, to), device_id_type=MESH)

    for p in range(1, n_grp):
        to = lax.rem(grp + p, n_grp)
        for n in range(len(spans)):
            cols = pl.ds(*spans[n][:2])
            block[to, :, cols] = total[to, :, cols].astype(block.dtype)
            give(p, n).start()
    block[grp] = total[grp].astype(block.dtype)
    keep = pltpu.make_async_copy(block.at[grp], out.at[grp], own_sem.at[2])
    keep.start()

    for dz, source, colour, ways in sent:
        def drain(source=source, colour=colour, ways=ways):
            for way in ways:
                when(edges[way], copy(source, colour, way).wait_send)
        if ways:
            when(valid(dz), drain)
    for p in range(1, n_grp):
        half_copy(p).wait_send()
    for o in range(1, n_aux):
        fac_copy(o).wait_send()
    for o in range(n_aux):
        source = lax.rem(me + n_aux - o, n_aux)
        for p in range(1, n_grp):
            share(o, source, p).wait_send()
    for p in range(1, n_grp):
        giver = lax.rem(grp + n_grp - p, n_grp)
        for n in range(len(spans)):
            cols = pl.ds(*spans[n][:2])
            give(p, n).wait_send()
            pltpu.make_async_remote_copy(
                src_ref=block.at[giver, :, cols], dst_ref=out.at[giver, :, cols],
                send_sem=osend.at[p, n], recv_sem=orecv.at[p, n],
                device_id=(me, giver), device_id_type=MESH).wait_recv()
    keep.wait()


def panels_any(integrals, pairs, occ, virtual, stored, n_aux, n_grp):
    depth = stored.shape[0]
    width = stored.shape[1] // n_grp
    aux_rows, nb, flat = integrals.shape
    nocc, nblocks, blk = occ.shape
    nbas, slab = virtual.shape
    pieces = len(spans_of(width))
    cols = nocc * (slab // n_aux)
    dma = pltpu.SemaphoreType.DMA
    hbm = pl.BlockSpec(memory_space=pltpu.HBM)
    vmem = pl.BlockSpec(memory_space=pltpu.VMEM)
    return pl.pallas_call(
        functools.partial(panel_any_kernel, n_aux, n_grp),
        out_shape=jax.ShapeDtypeStruct((n_grp, cols, width), jnp.bfloat16),
        in_specs=[hbm, vmem, vmem, hbm, hbm],
        out_specs=hbm,
        scratch_shapes=[
            pltpu.VMEM((n_aux, depth, width), jnp.bfloat16),
            pltpu.VMEM((n_grp, n_aux, depth, cols), jnp.bfloat16),
            pltpu.VMEM((n_grp, cols, width), jnp.float32),
            pltpu.VMEM((n_grp, cols, width), jnp.bfloat16),
            pltpu.VMEM(integrals.shape, jnp.bfloat16),
            pltpu.VMEM(virtual.shape, jnp.bfloat16),
            pltpu.VMEM((nocc, nb, flat), jnp.float32),
            pltpu.VMEM((nocc * aux_rows, nb, LANES), jnp.float32),
            pltpu.VMEM((nb, nocc * aux_rows, LANES), jnp.float32),
            pltpu.VMEM((n_grp, nocc * aux_rows, nbas), jnp.bfloat16),
            pltpu.VMEM((n_aux, depth, cols), jnp.bfloat16),
            dma((5,)),
            dma((pieces, n_aux)),
            dma((pieces, 4, n_aux)),
            dma((n_aux,)),
            dma((n_aux,)),
            dma((n_grp, n_aux)),
            dma((n_grp, n_aux)),
            dma((n_grp, pieces)),
            dma((n_grp, pieces)),
            dma((n_grp,)),
            dma((n_grp,)),
        ],
        compiler_params=pltpu.CompilerParams(
            collective_id=0, has_side_effects=True, vmem_limit_bytes=63 * 1024 * 1024),
    )(integrals, pairs, occ, virtual, stored)


HALVE, OWN, OTHER, FACTOR, CROSS, TURN, STORED, FINISH = range(8)
JOINT = 0.67
TUNED = (
    (6, 1, 0, 0), (6, 3, 0, 0), (0,), (6, 5, 0, 0), (6, 1, 1, 0), (6, 0, 0, 0), (6, 2, 0, 1), (6, 3, 1, 0), (1,),
    (6, 1, 2, 0), (6, 1, 0, 1), (6, 5, 0, 1), (6, 2, 0, 0), (6, 3, 0, 1), (6, 1, 3, 0), (6, 3, 2, 0), (2,),
    (6, 2, 1, 0), (6, 5, 1, 1), (6, 1, 1, 1), (6, 3, 3, 0), (3, 0), (3, 2), (3, 3), (3, 5), (3, 4), (6, 3, 1, 1),
    (4, 0), (6, 2, 2, 0), (3, 6), (4, 3), (6, 2, 3, 0), (6, 5, 1, 0), (3, 1), (3, 7), (6, 0, 0, 1), (4, 2),
    (6, 1, 2, 1), (6, 2, 1, 1), (6, 1, 3, 1), (6, 5, 2, 0), (6, 3, 2, 1), (6, 5, 2, 1), (6, 4, 0, 0), (4, 5), (4, 1),
    (6, 2, 2, 1), (6, 5, 3, 0), (4, 6), (4, 4), (6, 3, 3, 1), (6, 0, 1, 0), (6, 0, 1, 1), (6, 4, 0, 1), (4, 7),
    (6, 5, 3, 1), (5,), (7, 1), (6, 0, 2, 0), (6, 0, 2, 1), (6, 4, 1, 1), (6, 0, 3, 0), (7, 3), (6, 2, 3, 1),
    (6, 4, 1, 0), (6, 0, 3, 1), (6, 4, 2, 1), (7, 5), (7, 2), (6, 4, 2, 0), (6, 4, 3, 0), (6, 4, 3, 1), (7, 0),
    (7, 4),
)


def plan(pieces, line, n_pairs):
    stored = [(STORED, n, hop, far) for hop in range(line) for far in (0, 1) for n in range(pieces + 2)]
    factor = [(kind, o) for kind in (FACTOR, CROSS) for o in range(n_pairs)]
    plain = [(HALVE,), (OWN,), (OTHER,)] + stored + factor + [(TURN,)] + [(FINISH, n) for n in range(pieces + 2)]
    return TUNED if sorted(TUNED) == sorted(plain) else plain


def weigh_blocks(pairs, occ, weights):
    nocc, nbas = occ.shape
    nb = pairs.shape[1]
    blk = math.isqrt(weights.shape[2])
    per = LANES // blk
    tiles = nbas // LANES
    line = lax.broadcasted_iota(jnp.int32, (tiles, nb), 0) * per
    step = 8 * LANES
    row = lax.broadcasted_iota(jnp.int32, (blk, step), 0) * blk
    col = lax.broadcasted_iota(jnp.int32, (blk, step), 1)
    orbital = occ[...].astype(jnp.float32)
    for i in range(nocc):
        table = jnp.concatenate(
            [orbital[i:i + 1, t * LANES:(t + 1) * LANES] for t in range(tiles)], axis=0).astype(jnp.bfloat16)
        picked = None
        for f in range(per):
            pick = (pairs[0:1, :] == line + f).astype(jnp.bfloat16)
            term = lax.dot_general(
                pick, table[:, f * blk:(f + 1) * blk], (((0,), (0,)), ((), ())), preferred_element_type=jnp.float32)
            picked = term if picked is None else picked + term
        picked = picked.astype(jnp.bfloat16)
        for t in range(weights.shape[2] // step):
            offset = col + t * step - row
            spread = ((offset >= 0) & (offset < blk)).astype(jnp.bfloat16)
            weights[i, :, t * step:(t + 1) * step] = jnp.dot(
                picked, spread, preferred_element_type=jnp.float32)


def contract_rows(blk, integrals, weights, part, low, high):
    aux_rows = integrals.shape[0]
    nocc = weights.shape[0]

    @pl.loop(low, high)
    def _(p):
        for i in range(nocc):
            sums = [None, None]
            for t in range(integrals.shape[2] // LANES):
                cols = slice(t * LANES, (t + 1) * LANES)
                term = integrals[p, :, cols].astype(jnp.float32) * weights[i, :, cols]
                sums[t % 2] = term if sums[t % 2] is None else sums[t % 2] + term
            total = sums[0] + sums[1]
            whole = total
            for f in range(1, LANES // blk):
                whole = whole + pltpu.roll(total, f * blk, 1)
            part[i * aux_rows + p] = whole


def compact(blk, part, half, grp):
    nb = part.shape[1]
    per = LANES // blk
    lane = lax.broadcasted_iota(jnp.int32, (part.shape[0], LANES), 1) // blk
    for t in range(nb // per):
        tile = part[:, t * per, :]
        for f in range(1, per):
            tile = jnp.where(lane == f, part[:, t * per + f, :], tile)
        half[grp, :, t * LANES:(t + 1) * LANES] = tile.astype(half.dtype)


def expand(nocc, local, q, index, half, virt, chunk):
    n_grp, both, depth = half.shape
    blk = virt.shape[1]
    aux_rows = both // nocc
    wide = 2 * local
    step = math.lcm(wide, 2 * LANES)
    top = pl.ds(pl.multiple_of(q * aux_rows, aux_rows), aux_rows)
    for t in range(virt.shape[2] // step):
        cols = slice(t * step, (t + 1) * step)
        right = jnp.concatenate([virt[index[q, 1, k], :, cols] for k in range(depth // blk)], axis=0)
        product = jnp.dot(half[q], right, preferred_element_type=jnp.float32).astype(chunk.dtype)
        for c in range(step // wide):
            for i in range(nocc):
                chunk[t * (step // wide) + c, top, i * wide:(i + 1) * wide] = product[
                    i * aux_rows:(i + 1) * aux_rows, c * wide:(c + 1) * wide]


def panel_kernel(n_aux, v, integrals, pairs_in, occ_in, virtual, stored, out, rows, wides, fac, turned, block, slab,
                 ints, virt, weights, part, half, chunk, pairs, index, occ,
                 load_sem, own_sem, xsend, xrecv, send, recv, own_wide, xsend_wide, xrecv_wide, send_wide, recv_wide,
                 hsend, hrecv, fsend, frecv, gsend, grecv, psend, precv, osend, orecv, wsend, wrecv):
    me = lax.axis_index("aux")
    grp = lax.axis_index("grp")
    other = 1 - grp
    line = n_aux // PLANE
    nj = stored.shape[1] // v
    pieces = rows.shape[0]
    piece = rows.shape[3] // nj
    wide = wides.shape[3] // nj
    base = 4 * pieces * piece
    nocc = occ.shape[0]
    blk = virtual.shape[1]
    aux_rows = integrals.shape[0]
    local = virtual.shape[2] // n_aux
    z = me // PLANE
    x = me % 2
    y = (me // 2) % 2
    pair = me // 2
    n_pairs = n_aux // 2
    xmate = me + 1 - 2 * x
    ymate = me + 2 * (1 - 2 * y)
    edges = {"up": z + 1 < line, "down": z >= 1, "x": None, "y": None}
    targets = {"up": me + PLANE, "down": me - PLANE, "x": xmate, "y": ymate}
    slots = {"up": 0, "down": 1, "x": 2, "y": 2}
    mine = 2 * x + grp
    theirs = 2 * (1 - x) + grp

    def column(j, q, n):
        return pl.ds(pl.multiple_of(j * v + (q * pieces + n) * piece, LANES), piece)

    def column_wide(j, core, n):
        return pl.ds(pl.multiple_of(j * v + base + (core * 2 + n) * wide, LANES), wide)

    narrow = dict(
        ref=rows, width=piece, own=own_sem, xsend=xsend, xrecv=xrecv, send=send, recv=recv, mate=xmate, last="y",
        here=lambda j, n: column(j, mine, n), there=lambda j, n: column(j, theirs, n))
    broad = [dict(
        ref=wides, width=wide, own=own_wide, xsend=xsend_wide, xrecv=xrecv_wide, send=send_wide, recv=recv_wide,
        mate=mate, last=last, here=lambda j, n: column_wide(j, grp, n), there=lambda j, n: column_wide(j, grp, n))
        for mate, last in ((xmate, "y"), (ymate, "x"))]
    every = [(narrow, n) for n in range(pieces)] + [(broad[n], n) for n in range(2)]

    def at_of(kind, n, source, j):
        return kind["ref"].at[n, source, :, pl.ds(j * kind["width"], kind["width"])]

    def own_copy(kind, n, j):
        return pltpu.make_async_copy(stored.at[:, kind["here"](j, n)], at_of(kind, n, me, j), kind["own"].at[n, j])

    load_pairs = pltpu.make_async_copy(pairs_in.at[0], pairs.at[grp], load_sem.at[0])
    load_pairs.start()
    load_occ = pltpu.make_async_copy(occ_in, occ, load_sem.at[1])
    load_occ.start()
    load_index = pltpu.make_async_copy(pairs_in.at[0], index.at[grp], load_sem.at[4])
    load_index.start()
    load_ints = pltpu.make_async_copy(integrals, ints, load_sem.at[2])
    load_ints.start()
    for kind, n in every:
        for j in range(nj):
            own_copy(kind, n, j).start()
    load_virt = pltpu.make_async_copy(virtual, virt, load_sem.at[3])
    load_virt.start()

    barrier = pltpu.get_barrier_semaphore()
    peers = [((pair + o) % n_pairs * 2 + x, grp) for o in range(1, n_pairs)]
    peers += [(xmate, grp), (xmate, other), (me, other)]
    for peer in peers:
        pl.semaphore_signal(barrier, inc=1, device_id=peer, device_id_type=MESH)

    def when(condition, action):
        if condition is None:
            action()
        else:
            pl.when(condition)(action)

    def remote(src, dst, send_sem, recv_sem, device):
        return pltpu.make_async_remote_copy(
            src_ref=src, dst_ref=dst, send_sem=send_sem, recv_sem=recv_sem, device_id=device, device_id_type=MESH)

    def copy(kind, n, source, way):
        at = kind["ref"].at[n, source]
        return remote(
            at, at, kind["send"].at[n, slots[way], source], kind["recv"].at[n, source], (targets[way], grp))

    def cross(kind, n, j):
        return remote(
            stored.at[:, kind["there"](j, n)], at_of(kind, n, me, j),
            kind["xsend"].at[n, j], kind["xrecv"].at[n, j], (kind["mate"], grp))

    def cross_wait(kind, n, j):
        at = at_of(kind, n, kind["mate"], j)
        remote(at, at, kind["xsend"].at[n, j], kind["xrecv"].at[n, j], (kind["mate"], grp)).wait_recv()

    def valid(dz):
        if dz == 0:
            return None
        return z - dz >= 0 if dz > 0 else z - dz < line

    sent = []

    def forward(kind, n, dz, far):
        source = (kind["mate"] if far else me) - dz * PLANE
        last = kind["last"]
        ways = ("up", "down", last) if dz == 0 else (("up", last) if dz > 0 else ("down", last))
        sent.append((kind, n, dz, source, ways))

        def act():
            if dz == 0:
                for j in range(nj):
                    if far:
                        cross_wait(kind, n, j)
                    else:
                        own_copy(kind, n, j).wait()
            else:
                copy(kind, n, source, last).wait_recv()
            for way in ways:
                when(edges[way], copy(kind, n, source, way).start)

        when(valid(dz), act)

    def stage(group, distance, *fars):
        for kind, n in group:
            for far in fars:
                for dz in sorted({distance, -distance}):
                    forward(kind, n, dz, far)

    def half_copy():
        return remote(half.at[grp], half.at[grp], hsend.at[0], hrecv.at[0], (me, other))

    def pairs_copy():
        return remote(pairs.at[grp], pairs.at[grp], hsend.at[1], hrecv.at[1], (me, other))

    def fac_copy(o):
        to = (pair + o) % n_pairs
        return remote(chunk.at[to], fac.at[grp, me], fsend.at[o], frecv.at[o], (to * 2 + x, grp))

    def fac_source(o):
        return (pair + n_pairs - o) % n_pairs * 2

    def fac_cross(o):
        source = fac_source(o) + x
        return remote(fac.at[grp, source], fac.at[grp, source], gsend.at[o], grecv.at[o], (xmate, grp))

    def share(o, far):
        source = fac_source(o) + (1 - x if far else x)
        return remote(
            fac.at[grp, source], fac.at[grp, source], psend.at[int(far), o], precv.at[int(far), o], (me, other))

    def give(n, rel, q, j):
        to = (grp + q) % 2
        chip = 1 - x if rel else x
        src = block.at[n, to, chip]
        dst = out.at[:, :, column(0, mine, n)]
        if not rel and not q:
            return pltpu.make_async_copy(src, dst, osend.at[n, 0, j])
        return remote(
            src, dst, osend.at[n, 2 * rel + q, j], orecv.at[n, 2 * rel + q, j], (xmate if rel else me, to))

    def taken(n, rel, q, j):
        source = 2 * (1 - x if rel else x) + (grp + q) % 2
        return remote(
            block.at[n, 0, 0], out.at[:, :, column(0, source, n)],
            osend.at[n, 2 * rel + q, j], orecv.at[n, 2 * rel + q, j], (xmate, grp))

    def pass_over(n, q, j):
        to = (grp + q) % 2
        src = slab.at[n, to]
        dst = out.at[:, :, column_wide(0, grp, n)]
        if not q:
            return pltpu.make_async_copy(src, dst, wsend.at[n, q, j])
        return remote(src, dst, wsend.at[n, q, j], wrecv.at[n, j], (me, to))

    def passed(n, j):
        return remote(
            slab.at[n, 0], out.at[:, :, column_wide(0, other, n)],
            wsend.at[n, 1, j], wrecv.at[n, j], (me, other))

    def arrivals(kind, n):
        mate = ymate if kind["last"] == "y" else xmate
        for dz in range(1 - line, line):
            for far in (0, 1):
                step = (kind["mate"] - me) if far else 0

                def arrive(source=mate + step - dz * PLANE):
                    copy(kind, n, source, kind["last"]).wait_recv()

                when(valid(dz), arrive)

    def finish(n):
        arrivals(narrow, n)
        right = rows[n].reshape(-1, nj * piece)
        for q in range(2):
            left = turned[q].reshape(-1, right.shape[0])
            term = jnp.dot(left, right, preferred_element_type=jnp.float32).astype(block.dtype)
            for chip in range(2):
                for j in range(nj):
                    block[n, q, chip, :, j, :] = term[
                        chip * nocc * local:(chip + 1) * nocc * local, j * piece:(j + 1) * piece]
        for rel, q in ((1, 0), (1, 1), (0, 1), (0, 0)):
            give(n, rel, q, 0).start()

    def finish_wide(n):
        arrivals(broad[n], n)
        tile = math.gcd(2 * LANES, wide)
        for q in (1, 0):
            to = (grp + q) % 2
            for t in range(nj * wide // tile):
                cols = slice(t * tile, (t + 1) * tile)
                right = wides[n, :, :, cols].reshape(-1, tile)
                j, start = t * tile // wide, t * tile % wide
                slab[n, to, :, j, start:start + tile] = jnp.dot(
                    turned[to, x], right, preferred_element_type=jnp.float32).astype(slab.dtype)
            pass_over(n, q, 0).start()

    def wait_fac(o):
        if o:
            source = fac_source(o) + x
            remote(fac.at[grp, source], fac.at[grp, source], fsend.at[o], frecv.at[o], (source, grp)).wait_recv()
        else:
            keep.wait()
        fac_cross(o).start()
        share(o, False).start()

    def wait_cross(o):
        source = fac_source(o) + 1 - x
        remote(fac.at[grp, source], fac.at[grp, source], gsend.at[o], grecv.at[o], (xmate, grp)).wait_recv()
        share(o, True).start()

    def halve():
        contract_rows(blk, ints, weights, part, aux_rows // 2, aux_rows)
        compact(blk, part, half, grp)
        half_copy().start()

    def expand_own():
        load_index.wait()
        load_virt.wait()
        expand(nocc, local, grp, index, half, virt, chunk)

    def expand_other():
        remote(pairs.at[other], pairs.at[other], hsend.at[1], hrecv.at[1], (me, other)).wait_recv()
        load_other = pltpu.make_async_copy(pairs.at[other], index.at[other], load_sem.at[0])
        load_other.start()
        load_other.wait()
        remote(half.at[other], half.at[other], hsend.at[0], hrecv.at[0], (me, other)).wait_recv()
        expand(nocc, local, other, index, half, virt, chunk)
        for o in range(1, n_pairs):
            fac_copy(o).start()
        keep.start()

    def turn():
        for far in (False, True):
            for o in range(n_pairs):
                at = fac.at[other, fac_source(o) + (1 - x if far else x)]
                remote(at, at, psend.at[int(far), o], precv.at[int(far), o], (me, other)).wait_recv()
        group = LANES // fac.shape[2]
        for q in range(2):
            for t in range(n_aux // group):
                tall = fac[q, t * group:(t + 1) * group].reshape(LANES, -1).T
                for i in range(nocc):
                    for chip in range(2):
                        top = (i * 2 + chip) * local
                        turned[q, chip, i * local:(i + 1) * local, t * LANES:(t + 1) * LANES] = tall[top:top + local]

    keep = pltpu.make_async_copy(chunk.at[pair], fac.at[grp, me], load_sem.at[1])
    load_pairs.wait()
    load_occ.wait()
    weigh_blocks(pairs[grp], occ, weights)
    load_ints.wait()
    contract_rows(blk, ints, weights, part, 0, aux_rows // 2)
    pl.semaphore_wait(barrier, len(peers))
    pairs_copy().start()
    for kind, n in every:
        for j in range(nj):
            cross(kind, n, j).start()
    steps = {
        HALVE: halve, OWN: expand_own, OTHER: expand_other, FACTOR: wait_fac, CROSS: wait_cross, TURN: turn,
        STORED: lambda n, hop, far: stage([every[n]], hop, far),
        FINISH: lambda n: finish(n) if n < pieces else finish_wide(n - pieces)}
    for step, *operands in plan(pieces, line, n_pairs):
        steps[step](*operands)

    for kind, n, dz, source, ways in sent:
        def drain(kind=kind, n=n, source=source, ways=ways):
            for way in ways:
                when(edges[way], copy(kind, n, source, way).wait_send)
        when(valid(dz), drain)
    for kind, n in every:
        for j in range(nj):
            cross(kind, n, j).wait_send()
    half_copy().wait_send()
    pairs_copy().wait_send()
    for o in range(n_pairs):
        if o:
            fac_copy(o).wait_send()
        fac_cross(o).wait_send()
        share(o, False).wait_send()
        share(o, True).wait_send()
    for n in range(pieces):
        for j in range(1):
            for rel, q in ((1, 0), (1, 1), (0, 1)):
                give(n, rel, q, j).wait_send()
                taken(n, rel, q, j).wait_recv()
            give(n, 0, 0, j).wait()
    for n in range(2):
        for j in range(1):
            pass_over(n, 1, j).wait_send()
            passed(n, j).wait_recv()
            pass_over(n, 0, j).wait()


def panels(integrals, pairs, occupied, virtual, stored, n_aux, v):
    depth = stored.shape[0]
    aux_rows, nb, flat = integrals.shape
    nocc = occupied.shape[0]
    blk = math.isqrt(flat)
    slab = virtual.shape[2]
    nj = stored.shape[1] // v
    piece = LANES
    pieces = round(v // (4 * piece) * JOINT)
    wide = (v - 4 * pieces * piece) // 4
    cols = nocc * (slab // n_aux)
    n_pairs = n_aux // 2
    dma = pltpu.SemaphoreType.DMA
    hbm = pl.BlockSpec(memory_space=pltpu.HBM)
    return pl.pallas_call(
        functools.partial(panel_kernel, n_aux, v),
        out_shape=jax.ShapeDtypeStruct((cols, nj, v), jnp.bfloat16),
        in_specs=[hbm] * 5,
        out_specs=hbm,
        scratch_shapes=[
            pltpu.VMEM((pieces, n_aux, depth, nj * piece), jnp.bfloat16),
            pltpu.VMEM((2, n_aux, depth, nj * wide), jnp.bfloat16),
            pltpu.VMEM((2, n_aux, depth, 2 * cols), jnp.bfloat16),
            pltpu.VMEM((2, 2, cols, n_aux * depth), jnp.bfloat16),
            pltpu.VMEM((pieces, 2, 2, cols, nj, piece), jnp.bfloat16),
            pltpu.VMEM((2, 2, cols, nj, wide), jnp.bfloat16),
            pltpu.VMEM(integrals.shape, jnp.bfloat16),
            pltpu.VMEM(virtual.shape, jnp.bfloat16),
            pltpu.VMEM((nocc, nb, flat), jnp.float32),
            pltpu.VMEM((nocc * aux_rows, nb, LANES), jnp.float32),
            pltpu.VMEM((2, nocc * aux_rows, nb * blk), jnp.bfloat16),
            pltpu.VMEM((n_pairs, depth, 2 * cols), jnp.bfloat16),
            pltpu.VMEM((2, 2, nb), jnp.int32),
            pltpu.SMEM((2, 2, nb), jnp.int32),
            pltpu.VMEM(occupied.shape, jnp.bfloat16),
            dma((5,)),
            dma((pieces, nj)),
            dma((pieces, nj)),
            dma((pieces, nj)),
            dma((pieces, 3, n_aux)),
            dma((pieces, n_aux)),
            dma((2, nj)),
            dma((2, nj)),
            dma((2, nj)),
            dma((2, 3, n_aux)),
            dma((2, n_aux)),
            dma((2,)),
            dma((2,)),
            dma((n_pairs,)),
            dma((n_pairs,)),
            dma((n_pairs,)),
            dma((n_pairs,)),
            dma((2, n_pairs)),
            dma((2, n_pairs)),
            dma((pieces, 4, nj)),
            dma((pieces, 4, nj)),
            dma((2, 2, nj)),
            dma((2, nj)),
        ],
        compiler_params=pltpu.CompilerParams(
            collective_id=0, has_side_effects=True, vmem_limit_bytes=63 * 1024 * 1024),
    )(integrals, pairs, occupied, virtual, stored)


def make_per_device(n_aux, n_grp, v):
    def per_device(integrals, block_pairs, occupied, virtual, stored):
        nocc, nbas = occupied.shape
        local = virtual.shape[1] // n_aux
        blk = math.isqrt(integrals.shape[2])
        if n_grp == 2 and n_aux % PLANE == 0 and v % (4 * LANES) == 0 and LANES % stored.shape[0] == 0:
            panel = panels(integrals, block_pairs.transpose(0, 2, 1), occupied,
                           virtual.reshape(nbas // blk, blk, -1), stored, n_aux, v)
            return panel.reshape(nocc, local, panel.shape[1], v)
        occ = occupied.reshape(nocc, nbas // blk, blk)
        panel = panels_any(integrals, block_pairs, occ, virtual, stored, n_aux, n_grp)
        return panel.transpose(1, 0, 2).reshape(nocc, local, n_grp * panel.shape[2] // v, v)

    return per_device


def solution(mesh):
    n_aux, n_grp = mesh.shape["aux"], mesh.shape["grp"]

    def whole(integrals, block_pairs, occupied, virtual, stored):
        return jax.shard_map(
            make_per_device(n_aux, n_grp, virtual.shape[1]),
            mesh=mesh,
            in_specs=(
                P(("aux", "grp"), None, None),
                P(("aux", "grp"), None, None),
                P(),
                P(None, "grp"),
                P("aux", None),
            ),
            out_specs=P(None, ("grp", "aux"), None, None),
            check_vma=False,
        )(integrals, block_pairs, occupied, virtual, stored)

    return whole
```
